512 devices in a mesh: wide: 32 (over x, z_lo, core), oct: 16 (over y, z_hi).
Axes of the slice: x: 4, y: 4, z: 16 (z_hi: 4, z_lo: 4; z = z_hi * 4 + z_lo), core: 2. Of those that a mesh axis runs over, the one named last changes fastest.
Arguments:
- positions: float32 [3, 1048576], P(None, ('wide', 'oct'))
- masses: float32 [1048576], P(('wide', 'oct')), may hold values from 0.5 to 2
- counts: int32 [4096], P(('wide', 'oct')), may hold values from 64 to 256, as said below
- near_list: int32 [4096, 8], P(('wide', 'oct')), may hold values from 0 to 79, as said below
- far_list: int32 [4096, 16], P(('wide', 'oct')), may hold values from 0 to 767, as said below
Outputs:
- acceleration: float32 [3, 1048576], P(None, ('wide', 'oct'))
The draws below stay inside these ranges and needn't reach their ends.
Inputs may be any that keep to these rules, and one draw needn't show every extreme that they name: counts lie between 64 and 256; both ends are reached. `near_list`: on every device the lists of its blocks together name every level 0 to 9; two entries of one block never name the same block. `far_list`: on every device the lists of its blocks together name every wide level 0 to 5.
All inputs are finite; a program needn't handle non-finite values.
Results may differ from the reference program's by a relative error of at most 0.0003.
Values sent between devices are 32-bit elements; how exact they have to be, the bound alone decides.
No kernel may reach another device: no remote copies, remote signals or barrier semaphores. Data moves between devices by JAX's collectives and lax.ppermute only.
A program may use at most 64 MiB of HBM per device.

```python
import math
import jax
import jax.numpy as jnp
from jax import lax

LEAF = 256
BLK_DEV = 8
NEAR = 8
FAR = 16
WIDE_BITS = 5
LEVELS = 9
BLOCKS = 4096
BODIES = 1048576
N_WIDE = 32
N_OCT = 16


def draw_positions(key, part):
    key_one, key_two = jax.random.split(key)
    centres = jax.random.uniform(key_one, (3, BLOCKS, 1), jnp.float32, -2.0, 2.0)
    offsets = jnp.clip(0.5 * jax.random.normal(key_two, (3, BLOCKS, LEAF), jnp.float32), -2.0, 2.0)
    return (centres + offsets).reshape(3, BODIES)


def draw_counts(key, part):
    key_one, key_two, key_three = jax.random.split(jax.random.fold_in(key, 11), 3)
    counts = jax.random.randint(key_one, (BLOCKS,), LEAF // 4, LEAF + 1)
    full_index = jax.random.randint(key_two, (), 0, BLOCKS)
    low_index = (full_index + 1 + jax.random.randint(key_three, (), 0, BLOCKS - 1)) % BLOCKS
    counts = counts.at[full_index].set(LEAF)
    counts = counts.at[low_index].set(LEAF // 4)
    return counts.astype(jnp.int32)


def device_levels(key, sets_count, entries):
    devices = N_WIDE * N_OCT
    keys_all = jax.random.split(key, devices)
    orders = jax.vmap(lambda single: jax.random.permutation(single, sets_count))(keys_all)
    block_index = jnp.arange(BLOCKS, dtype=jnp.int32)
    local = block_index % BLK_DEV
    entry_index = jnp.arange(entries, dtype=jnp.int32)
    position = (local[:, None] + entry_index[None, :]) % sets_count
    rows_order = orders[block_index // BLK_DEV]
    return jnp.take_along_axis(rows_order, position, axis=1).astype(jnp.int32)


def draw_near_list(key, part):
    key_one, key_two = jax.random.split(jax.random.fold_in(key, 23))
    sets_count = LEVELS + 1
    level_index = device_levels(key_one, sets_count, NEAR)
    base_slot = jax.random.randint(key_two, (BLOCKS, sets_count), 0, BLK_DEV)
    entry_index = jnp.arange(NEAR, dtype=jnp.int32)
    slot_index = (jnp.take_along_axis(base_slot, level_index, axis=1) + entry_index[None, :] // sets_count) % BLK_DEV
    return (level_index * BLK_DEV + slot_index).astype(jnp.int32)


def draw_far_list(key, part):
    key_one, key_two, key_three = jax.random.split(jax.random.fold_in(key, 37), 3)
    sets_count = WIDE_BITS + 1
    level_index = device_levels(key_one, sets_count, FAR)
    member = jax.random.randint(key_two, (BLOCKS, FAR), 0, N_OCT)
    slot_index = jax.random.randint(key_three, (BLOCKS, FAR), 0, BLK_DEV)
    return (level_index * (N_OCT * BLK_DEV) + member * BLK_DEV + slot_index).astype(jnp.int32)


def shard_levels(key, shape, shards, least, top_value):
    level = 1.0
    for axis_at, blocks in shards:
        draws = jax.random.uniform(jax.random.fold_in(jax.random.fold_in(key, 6), axis_at), (blocks,), jnp.float32, least / len(shards), top_value / len(shards))
        level = level * jnp.repeat(jnp.exp(draws), shape[axis_at] // blocks).reshape((-1,) + (1,) * (len(shape) - 1 - axis_at))
    return level


def setup_inputs(seed: int = 0) -> dict:
    key_list = jax.random.split(jax.random.key(seed), 6)
    return {
        "positions": draw_positions(jax.random.fold_in(key_list[5], 71), 0),
        "masses": jnp.clip(jnp.exp(math.log(2.0) - 1.3862944 * jax.random.uniform(key_list[1], (BODIES,), jnp.float32) ** shard_levels(key_list[1], (BODIES,), ((0, 512),), -0.2, 0.2)), 0.5, 2.0),
        "counts": draw_counts(jax.random.fold_in(key_list[5], 71), 0),
        "near_list": draw_near_list(jax.random.fold_in(key_list[5], 71), 0),
        "far_list": draw_far_list(jax.random.fold_in(key_list[5], 71), 0),
    }


near_soft = 0.01
far_soft = 0.25

def near_term(targets, sources, source_mass):
    delta = sources[:, :, None, :] - targets[:, :, :, None]
    dist_sq = lax.optimization_barrier(jnp.sum(delta * delta, axis=0)) + near_soft
    inverse = lax.rsqrt(dist_sq)
    weight = source_mass[:, None, :] * (inverse * inverse * inverse)
    return lax.optimization_barrier(jnp.sum(delta * weight[None], axis=3))

def cell_moments(block_pos, block_mass):
    total = lax.optimization_barrier(jnp.sum(block_mass, axis=1))
    centre = lax.optimization_barrier(jnp.sum(block_pos * block_mass[None], axis=2)) / total[None]
    offset = block_pos - centre[:, :, None]
    radius_sq = lax.optimization_barrier(jnp.sum(offset * offset, axis=0))
    trace_part = lax.optimization_barrier(jnp.sum(block_mass * radius_sq, axis=1))

    def second(first_axis, other_axis):
        return lax.optimization_barrier(jnp.sum(block_mass * 3.0 * offset[first_axis] * offset[other_axis], axis=1))
    return jnp.stack([total, centre[0], centre[1], centre[2], second(0, 0) - trace_part, second(1, 1) - trace_part, second(2, 2) - trace_part, second(0, 1), second(0, 2), second(1, 2)])

def far_term(targets, chosen):
    rel = targets[:, :, None, :] - chosen[1:4, :, :, None]
    dist_sq = lax.optimization_barrier(jnp.sum(rel * rel, axis=0)) + far_soft
    inverse = lax.rsqrt(dist_sq)
    inv_sq = inverse * inverse
    inv_three = inverse * inv_sq
    inv_five = inv_three * inv_sq
    inv_seven = inv_five * inv_sq
    quad = chosen[4:10][:, :, :, None]
    qr_x = quad[0] * rel[0] + quad[3] * rel[1] + quad[4] * rel[2]
    qr_y = quad[3] * rel[0] + quad[1] * rel[1] + quad[5] * rel[2]
    qr_z = quad[4] * rel[0] + quad[5] * rel[1] + quad[2] * rel[2]
    rqr = rel[0] * qr_x + rel[1] * qr_y + rel[2] * qr_z
    radial = -chosen[0][:, :, None] * inv_three - 2.5 * rqr * inv_seven
    accel = rel * radial[None] + jnp.stack([qr_x, qr_y, qr_z]) * inv_five[None]
    return lax.optimization_barrier(jnp.sum(accel, axis=2))

def level_flip(level_index):
    return jnp.where(level_index > 0, jnp.left_shift(jnp.int32(1), jnp.maximum(level_index - 1, 0)), 0).astype(jnp.int32)

def reference(positions, masses, counts, near_list, far_list):
    devices = N_WIDE * N_OCT
    grav = 1.0 / (NEAR * LEAF)
    valid_mask = (lax.broadcasted_iota(jnp.int32, (BLOCKS, LEAF), 1) < counts[:, None]).astype(jnp.float32)
    block_pos = positions.reshape(3, BLOCKS, LEAF)
    block_mass = masses.reshape(BLOCKS, LEAF) * valid_mask
    cells = cell_moments(block_pos, block_mass)
    group_cells = N_OCT * BLK_DEV

    def one_device(device):
        first = (device * BLK_DEV).astype(jnp.int32)
        targets = lax.dynamic_slice_in_dim(block_pos, first, BLK_DEV, 1)
        near_rows = lax.dynamic_slice_in_dim(near_list, first, BLK_DEV, 0)
        source_block = jnp.bitwise_xor(device, level_flip(near_rows // BLK_DEV)) * BLK_DEV + near_rows % BLK_DEV
        source_pos = block_pos[:, source_block]
        source_mass = block_mass[source_block]
        near_sum = jnp.zeros((3, BLK_DEV, LEAF), jnp.float32)
        for entry in range(NEAR):
            near_sum = near_sum + near_term(targets, source_pos[:, :, entry], source_mass[:, entry])
        far_rows = lax.dynamic_slice_in_dim(far_list, first, BLK_DEV, 0)
        remain = far_rows % group_cells
        wide_index = jnp.bitwise_xor(device // N_OCT, level_flip(far_rows // group_cells))
        cell_block = (wide_index * N_OCT + remain // BLK_DEV) * BLK_DEV + remain % BLK_DEV
        far_sum = far_term(targets, cells[:, cell_block])
        mask_dev = lax.dynamic_slice_in_dim(valid_mask, first, BLK_DEV, 0)
        return ((near_sum + far_sum) * grav * mask_dev[None]).reshape(3, BLK_DEV * LEAF)
    result = lax.map(one_device, jnp.arange(devices, dtype=jnp.int32))
    return jnp.transpose(result, (1, 0, 2)).reshape(3, BODIES)
```

```python
import functools

import jax
import jax.numpy as jnp
from jax import lax
from jax.experimental import pallas as pl
from jax.experimental.pallas import tpu as pltpu
from jax.sharding import PartitionSpec as P

near_soft = 0.01
far_soft = 0.25
BLK = 8
LEAF = 256
BODY_ROWS = BLK * 8
CELL_SLOT = 16
GROUPS = 4
F32 = jnp.float32
VMEM = pl.BlockSpec(memory_space=pltpu.VMEM)
SMEM = pl.BlockSpec(memory_space=pltpu.SMEM)


def planes(ref):
    halves = [ref[pl.ds(k, BLK, stride=8), :] for k in range(8)]
    return [jnp.concatenate(halves[2 * c : 2 * c + 2], axis=1) for c in range(4)]


def pack_kernel(counts_ref, pos_ref, mass_ref, out_ref):
    lane = lax.broadcasted_iota(jnp.int32, (1, 128), 1)
    for b in range(BLK):
        for half in range(2):
            for c in range(3):
                at = b * LEAF + half * 128
                row = b * 8 + c * 2 + half
                out_ref[row : row + 1, :] = pos_ref[c : c + 1, at : at + 128]
            row = b * 8 + 6 + half
            live = lane + half * 128 < counts_ref[b]
            out_ref[row : row + 1, :] = jnp.where(live, mass_ref[2 * b + half : 2 * b + half + 1, :], 0.0)
    x, y, z, m = planes(out_ref)

    def total(a):
        return jnp.sum(a, axis=1, keepdims=True)

    mass = total(m)
    cx, cy, cz = total(x * m) / mass, total(y * m) / mass, total(z * m) / mass
    dx, dy, dz = x - cx, y - cy, z - cz
    mx, my, mz = m * dx, m * dy, m * dz
    xx, yy, zz = total(mx * dx), total(my * dy), total(mz * dz)
    trace = xx + yy + zz
    columns = [
        mass,
        cx,
        cy,
        cz,
        3.0 * xx - trace,
        3.0 * yy - trace,
        3.0 * zz - trace,
        3.0 * total(mx * dy),
        3.0 * total(mx * dz),
        3.0 * total(my * dz),
    ]
    lanes = lax.broadcasted_iota(jnp.int32, (BLK, 128), 1)
    blocks = lax.broadcasted_iota(jnp.int32, (BLK, 128), 0)
    tile = jnp.zeros((BLK, 128), F32)
    for k, column in enumerate(columns):
        tile = jnp.where(lanes % CELL_SLOT == k, column, tile)
    row = jnp.sum(jnp.where(lanes // CELL_SLOT == blocks, tile, 0.0), axis=0, keepdims=True)
    rows = lax.broadcasted_iota(jnp.int32, (lax.axis_size("oct"), 128), 0)
    out_ref[BODY_ROWS:, :] = jnp.where(rows == lax.axis_index("oct"), row, 0.0)


def near_block(b, near_ref, counts_ref, source_ref, cols, acc_ref):
    tgt = [cols[c] for c in range(3)]

    def chunk(g, carry):
        start = pl.multiple_of(g * (8 * GROUPS), 8 * GROUPS)
        t = [
            [
                jnp.broadcast_to(tgt[c][pl.ds(start + 8 * i, 8), b : b + 1], (8, 128))
                for c in range(3)
            ]
            for i in range(GROUPS)
        ]

        def entry(v, acc):
            acc = list(acc)
            code = near_ref[b, v]
            for half in range(2):
                s = [
                    jnp.broadcast_to(source_ref[code, 2 * c + half : 2 * c + half + 1, :], (8, 128))
                    for c in range(4)
                ]
                for i in range(GROUPS):
                    dx, dy, dz = s[0] - t[i][0], s[1] - t[i][1], s[2] - t[i][2]
                    inv = lax.rsqrt(dx * dx + dy * dy + dz * dz + near_soft)
                    w = s[3] * (inv * inv * inv)
                    acc[3 * i] += dx * w
                    acc[3 * i + 1] += dy * w
                    acc[3 * i + 2] += dz * w
            return tuple(acc)

        zero = jnp.zeros((8, 128), F32)
        acc = lax.fori_loop(0, near_ref.shape[1], entry, (zero,) * (3 * GROUPS))
        for i in range(GROUPS):
            for c in range(3):
                acc_ref[c, pl.ds(start + 8 * i, 8), :] = acc[3 * i + c]
        return carry

    lax.fori_loop(0, (counts_ref[b] + 8 * GROUPS - 1) // (8 * GROUPS), chunk, 0)


def force_kernel(near_ref, far_ref, counts_ref, far_vec_ref, *refs):
    *sets, out_ref, source_ref, table_ref, chosen_ref, tx, ty, tz, acc_ref, near_out = refs
    own = sets[0]
    cells = [sets[0], *sets[5:]]
    for s, ref in enumerate(sets):
        for b in range(BLK):
            source_ref[s * BLK + b] = ref[b * 8 : b * 8 + 8, :]
    members = own.shape[0] - BODY_ROWS
    for g, ref in enumerate(cells):
        table_ref[g * members : (g + 1) * members, :] = ref[BODY_ROWS:, :]
    x, y, z, _ = planes(own)
    tx[...], ty[...], tz[...] = x.T, y.T, z.T
    acc_ref[...] = jnp.zeros_like(acc_ref)
    for b in range(BLK):
        near_block(b, near_ref, counts_ref, source_ref, (tx, ty, tz), acc_ref)
        ones = jnp.ones((8, 128), jnp.bfloat16)
        for c in range(3):
            a = acc_ref[c]
            hi = a.astype(jnp.bfloat16)
            rest = a - hi.astype(F32)
            mid = rest.astype(jnp.bfloat16)
            low = (rest - mid.astype(F32)).astype(jnp.bfloat16)
            dims = (((1,), (1,)), ((), ()))
            row = sum(lax.dot_general(ones, part, dims, preferred_element_type=F32) for part in (low, mid, hi))
            near_out[c, b : b + 1, :] = row[0:1]
    far_count = far_ref.shape[1]
    for v in range(far_count):
        for b in range(BLK):
            chosen_ref[v * BLK + b : v * BLK + b + 1, :] = table_ref[pl.ds(far_ref[b, v] // BLK, 1), :]
    sums = [near_out[c] for c in range(3)]
    for v in range(far_count):
        tile = chosen_ref[v * BLK : (v + 1) * BLK, :]
        slot = far_vec_ref[:, v : v + 1] % BLK
        for bit in range(3):
            shift = CELL_SLOT << bit
            moved = pltpu.roll(tile, 128 - shift, 1)
            tile = jnp.where((slot // (1 << bit)) % 2 == 1, moved, tile)
        mass, cx, cy, cz, xx, yy, zz, xy, xz, yz = (tile[:, k : k + 1] for k in range(10))
        rx, ry, rz = x - cx, y - cy, z - cz
        inv = lax.rsqrt(rx * rx + ry * ry + rz * rz + far_soft)
        inv2 = inv * inv
        inv3 = inv * inv2
        inv5 = inv3 * inv2
        inv7 = inv5 * inv2
        qx = xx * rx + xy * ry + xz * rz
        qy = xy * rx + yy * ry + yz * rz
        qz = xz * rx + yz * ry + zz * rz
        rqr = rx * qx + ry * qy + rz * qz
        radial = -mass * inv3 - 2.5 * rqr * inv7
        sums[0] += rx * radial + qx * inv5
        sums[1] += ry * radial + qy * inv5
        sums[2] += rz * radial + qz * inv5
    lane = lax.broadcasted_iota(jnp.int32, (1, LEAF), 1)
    grav = 1.0 / (near_ref.shape[1] * LEAF)
    for c in range(3):
        near_out[c] = sums[c] * grav
        for b in range(BLK):
            out_ref[c : c + 1, b * LEAF : (b + 1) * LEAF] = jnp.where(
                lane < counts_ref[b], near_out[c, b : b + 1, :], 0.0
            )


def exchange(payload, axis, flip):
    return lax.ppermute(payload, axis, [(i, flip(i)) for i in range(lax.axis_size(axis))])


def joined(bodies, cells, more):
    return jnp.concatenate([bodies[:BODY_ROWS], cells[BODY_ROWS:] + more[BODY_ROWS:]], axis=0)


RELAY = (3, 2, 1, 0)


def on_device(positions, masses, counts, near_list, far_list):
    wide_bits = lax.axis_size("wide").bit_length() - 1
    own = pl.pallas_call(
        pack_kernel,
        out_shape=jax.ShapeDtypeStruct((BODY_ROWS + lax.axis_size("oct"), 128), F32),
        in_specs=[SMEM, VMEM, VMEM],
        out_specs=VMEM,
        compiler_params=pltpu.CompilerParams(vmem_limit_bytes=4 << 20),
        name="pack",
    )(counts, positions, masses.reshape(16, 128))
    held = own
    y_one = exchange(held, "oct", lambda i: i ^ 4)
    held = joined(own, held, y_one)
    y_two = exchange(held, "oct", lambda i: i ^ 8)
    held = joined(own, held, y_two)
    z_one = exchange(held, "oct", lambda i: i ^ 1)
    held = joined(own, held, z_one)
    z_two = exchange(joined(z_one, held, jnp.zeros_like(held)), "oct", lambda i: (i & ~3) | RELAY[i & 3])
    held = joined(own, held, z_two)
    wide = [exchange(held, "wide", lambda i, bit=bit: i ^ (1 << bit)) for bit in range(wide_bits)]
    sets = [held, z_one, z_two, y_one, y_two, *wide]
    blocks = BLK * len(sets)
    return pl.pallas_call(
        force_kernel,
        out_shape=jax.ShapeDtypeStruct(positions.shape, F32),
        in_specs=[SMEM, SMEM, SMEM, VMEM] + [VMEM] * len(sets),
        out_specs=VMEM,
        scratch_shapes=[
            pltpu.VMEM((blocks, 8, 128), F32),
            pltpu.VMEM((lax.axis_size("oct") * (1 + wide_bits), 128), F32),
            pltpu.VMEM((BLK * far_list.shape[1], 128), F32),
            pltpu.VMEM((LEAF, BLK), F32),
            pltpu.VMEM((LEAF, BLK), F32),
            pltpu.VMEM((LEAF, BLK), F32),
            pltpu.VMEM((3, LEAF, 128), F32),
            pltpu.VMEM((3, BLK, LEAF), F32),
        ],
        compiler_params=pltpu.CompilerParams(vmem_limit_bytes=16 << 20),
        name="force",
    )(near_list, far_list, counts, far_list, *sets)


def solution(mesh):
    return jax.shard_map(
        on_device,
        mesh=mesh,
        in_specs=(
            P(None, ("wide", "oct")),
            P(("wide", "oct")),
            P(("wide", "oct")),
            P(("wide", "oct"), None),
            P(("wide", "oct"), None),
        ),
        out_specs=P(None, ("wide", "oct")),
        check_vma=False,
    )
```

```python
import jax
import jax.numpy as jnp
from jax import lax
from jax.experimental import pallas as pl
from jax.experimental.pallas import tpu as pltpu
from jax.sharding import PartitionSpec as P


near_soft = 0.01
far_soft = 0.25
BLK = 8
LEAF = 256
BODY = BLK * 8
SLOT = 16
GROUPS = 4
CHUNK = 8 * GROUPS
UNROLL = 2
F32 = jnp.float32
I32 = jnp.int32
VMEM = pl.BlockSpec(memory_space=pltpu.VMEM)
SMEM = pl.BlockSpec(memory_space=pltpu.SMEM)
HBM = pl.BlockSpec(memory_space=pltpu.HBM)
RELAY = (3, 2, 1, 0)


def planes(ref):
    half = [[ref[pl.ds(h * 4 + c, BLK, stride=8), :] for h in range(2)] for c in range(4)]
    return [jnp.concatenate(pair, axis=1) for pair in half]


def pack_kernel(counts_hbm, pos_hbm, mass_hbm, out_ref, counts_ref, pos_ref, mass_ref, sems):
    copies = [
        pltpu.make_async_copy(src, dst, sems.at[i])
        for i, (src, dst) in enumerate(((pos_hbm, pos_ref), (mass_hbm, mass_ref), (counts_hbm, counts_ref)))
    ]
    for copy in copies:
        copy.start()
    for copy in copies:
        copy.wait()
    lane = lax.broadcasted_iota(I32, (1, 128), 1)
    for b in range(BLK):
        for half in range(2):
            row = b * 8 + half * 4
            at = b * LEAF + half * 128
            for c in range(3):
                out_ref[row + c : row + c + 1, :] = pos_ref[c : c + 1, at : at + 128]
            live = lane + half * 128 < counts_ref[b]
            out_ref[row + 3 : row + 4, :] = jnp.where(live, mass_ref[2 * b + half : 2 * b + half + 1, :], 0.0)
    x, y, z, m = planes(out_ref)

    def total(a):
        return jnp.sum(a, axis=1, keepdims=True)

    mass = total(m)
    cx, cy, cz = total(x * m) / mass, total(y * m) / mass, total(z * m) / mass
    dx, dy, dz = x - cx, y - cy, z - cz
    mx, my, mz = m * dx, m * dy, m * dz
    xx, yy, zz = total(mx * dx), total(my * dy), total(mz * dz)
    trace = xx + yy + zz
    first = [mass, cx, cy, cz, 3.0 * xx - trace, 3.0 * yy - trace, 3.0 * zz - trace, 3.0 * total(mx * dy)]
    last = [3.0 * total(mx * dz), 3.0 * total(my * dz)]
    lanes = lax.broadcasted_iota(I32, (BLK, 128), 1)
    blocks = lax.broadcasted_iota(I32, (BLK, 128), 0)

    def cell_row(columns):
        tile = jnp.zeros((BLK, 128), F32)
        for k, column in enumerate(columns):
            tile = jnp.where(lanes % SLOT == k, column, tile)
        return jnp.sum(jnp.where(lanes // SLOT == blocks, tile, 0.0), axis=0, keepdims=True)

    rows = jnp.where(blocks == 0, cell_row(first), 0.0)
    out_ref[BODY:, :] = jnp.where(blocks == 1, cell_row(last), rows)


def join_kernel(*refs):
    *sets, out_ref = refs
    first = [ref[BODY : BODY + 1, :] for ref in sets]
    last = sum(pltpu.roll(jnp.broadcast_to(ref[BODY + 1 : BODY + 2, :], (8, 128)), 2 * g, 1) if g else jnp.broadcast_to(ref[BODY + 1 : BODY + 2, :], (8, 128)) for g, ref in enumerate(sets))
    at = lax.broadcasted_iota(I32, (8, 128), 0)
    tile = jnp.where(at == 3, last, 0.0)
    for g in range(0, len(sets), 2):
        pair = jnp.broadcast_to(first[g], (8, 128))
        if g + 1 < len(sets):
            pair = pair + pltpu.roll(jnp.broadcast_to(first[g + 1], (8, 128)), 8, 1)
        tile = jnp.where(at == g // 2, pair, tile)
    for k in range(out_ref.shape[0]):
        out_ref[k, :BODY, :] = sets[0][:BODY, :]
        out_ref[k, BODY:, :] = tile


def near_sums(near_ref, counts_ref, own, sets, local_of, scratch):
    source_ref, tx, ty, tz, acc_ref, list_ref = scratch
    lane8 = lax.broadcasted_iota(I32, (BLK, 128), 1)
    block8 = lax.broadcasted_iota(I32, (BLK, 128), 0)
    masks = []
    for s, body in enumerate(sets):
        for b in range(BLK):
            tile = body(b)
            source_ref[s * BODY + b * 8 : s * BODY + b * 8 + 8, :] = tile
        second = source_ref[pl.ds(s * BODY + 7, BLK, stride=8), :]
        bits = jnp.where((lane8 == 0) & (second > 0.0), jnp.left_shift(1, block8), 0)
        masks.append(jnp.sum(bits))
    empty = len(sets) * BODY
    source_ref[empty : empty + 8, :] = jnp.zeros((8, 128), F32)
    x, y, z, _ = planes(own)
    tx[...], ty[...], tz[...] = x.T, y.T, z.T
    lengths = []
    for b in range(BLK):
        n = jnp.int32(0)
        for v in range(near_ref.shape[1]):
            code = near_ref[b, v]
            local = local_of(code // BLK)
            row = local * BODY + (code % BLK) * 8
            mask = jnp.int32(0)
            for s in range(len(sets)):
                mask = jnp.where(local == s, masks[s], mask)
            list_ref[b, n] = row
            n = n + (local >= 0).astype(I32)
            list_ref[b, n] = row + 4
            n = n + ((local >= 0) & (jnp.right_shift(mask, code % BLK) % 2 == 1)).astype(I32)
        for i in range(UNROLL - 1):
            list_ref[b, n + i] = empty
        lengths.append(n)
    acc_ref[...] = jnp.zeros_like(acc_ref)
    for b in range(BLK):

        def chunk(g, carry, b=b):
            start = pl.multiple_of(g * CHUNK, CHUNK)
            t = [
                [jnp.broadcast_to(ref[pl.ds(start + 8 * i, 8), b : b + 1], (8, 128)) for ref in (tx, ty, tz)]
                for i in range(GROUPS)
            ]

            def pair(k, acc):
                acc = list(acc)
                for u in range(UNROLL):
                    row = list_ref[b, k * UNROLL + u]
                    s = [jnp.broadcast_to(source_ref[pl.ds(row + c, 1), :], (8, 128)) for c in range(4)]
                    for i in range(GROUPS):
                        dx, dy, dz = s[0] - t[i][0], s[1] - t[i][1], s[2] - t[i][2]
                        inv = lax.rsqrt(dx * dx + dy * dy + dz * dz + near_soft)
                        w = s[3] * (inv * inv * inv)
                        acc[3 * i] += dx * w
                        acc[3 * i + 1] += dy * w
                        acc[3 * i + 2] += dz * w
                return tuple(acc)

            zero = jnp.zeros((8, 128), F32)
            acc = lax.fori_loop(0, (lengths[b] + UNROLL - 1) // UNROLL, pair, (zero,) * (3 * GROUPS))
            for i in range(GROUPS):
                for c in range(3):
                    acc_ref[c, pl.ds(b * LEAF + start + 8 * i, 8), :] = acc[3 * i + c]
            return carry

        lax.fori_loop(0, (counts_ref[b] + CHUNK - 1) // CHUNK, chunk, 0)
    out = []
    lane = lax.broadcasted_iota(I32, (LEAF, BLK), 1)
    for c in range(3):
        columns = jnp.zeros((LEAF, BLK), F32)
        for b in range(BLK):
            part = jnp.sum(acc_ref[c, b * LEAF : (b + 1) * LEAF, :], axis=1, keepdims=True)
            columns = jnp.where(lane == b, part, columns)
        out.append(columns.T)
    return out


def block_of(ref):
    return lambda b: ref[b * 8 : b * 8 + 8, :]


def first_near_kernel(near_ref, counts_ref, own, *refs):
    wide, (out_ref, *scratch) = refs[:5], refs[5:]
    sums = near_sums(
        near_ref,
        counts_ref,
        own,
        [block_of(own), *map(block_of, wide)],
        lambda level: jnp.where(level == 0, 0, jnp.where(level >= 5, level - 4, -1)),
        scratch,
    )
    for c in range(3):
        out_ref[c] = sums[c]


def second_near_kernel(near_ref, counts_ref, own, z_one, y_all, before, out_ref, *scratch):
    y = lax.axis_index("oct") // 4

    def member(flip):
        return lambda b: y_all[y ^ flip, b * 8 : b * 8 + 8, :]

    sums = near_sums(
        near_ref,
        counts_ref,
        own,
        [block_of(z_one), member(1), member(2)],
        lambda level: jnp.where(level == 1, 0, jnp.where((level == 3) | (level == 4), level - 2, -1)),
        scratch,
    )
    for c in range(3):
        out_ref[c] = before[c] + sums[c]


def last_kernel(near_ref, far_ref, counts_ref, far_vec_ref, own, z_one, z_two, before, out_ref, table_ref, chosen_ref, rows_ref, *scratch):
    sums = near_sums(near_ref, counts_ref, own, [block_of(z_two)], lambda level: jnp.where(level == 2, 0, -1), scratch)
    for c in range(3):
        sums[c] = before[c] + sums[c]
    me = lax.axis_index("oct") % 4
    other = 3 - me
    n = z_one.shape[0] - BODY
    for place, rows in (
        (me, own[BODY:, :]),
        (me ^ 1, z_one[BODY:, :]),
        (other, z_two[BODY : BODY + n, :]),
        (other ^ 1, z_two[BODY + n :, :]),
    ):
        table_ref[pl.ds(pl.multiple_of(place * n, n), n), :] = rows
    members = lax.axis_size("oct")
    far_count = far_ref.shape[1]
    for v in range(far_count):
        for b in range(BLK):
            code = far_ref[b, v]
            member = code // BLK % members
            row = member % 4 * n + member // 4 * 4
            at = v * BLK + b
            chosen_ref[0, at : at + 1, :] = table_ref[pl.ds(row + code // (2 * BLK * members), 1), :]
            chosen_ref[1, at : at + 1, :] = table_ref[pl.ds(row + 3, 1), :]
    x, y, z, _ = planes(own)
    for v in range(far_count):
        code = far_vec_ref[:, v : v + 1]
        group = code // (BLK * members)
        tiles = []
        for part, shift_by in ((0, group % 2 * 8), (1, group * 2)):
            tile = chosen_ref[part, v * BLK : (v + 1) * BLK, :]
            shift = code % BLK * SLOT + shift_by
            for bit in (8, 16, 32, 64) if part == 0 else (2, 4, 8, 16, 32, 64):
                tile = jnp.where(shift // bit % 2 == 1, pltpu.roll(tile, 128 - bit, 1), tile)
            tiles.append(tile)
        mass, cx, cy, cz, xx, yy, zz, xy = (tiles[0][:, k : k + 1] for k in range(8))
        xz, yz = (tiles[1][:, k : k + 1] for k in range(2))
        rx, ry, rz = x - cx, y - cy, z - cz
        inv = lax.rsqrt(rx * rx + ry * ry + rz * rz + far_soft)
        inv2 = inv * inv
        inv3 = inv * inv2
        inv5 = inv3 * inv2
        inv7 = inv5 * inv2
        qx = xx * rx + xy * ry + xz * rz
        qy = xy * rx + yy * ry + yz * rz
        qz = xz * rx + yz * ry + zz * rz
        rqr = rx * qx + ry * qy + rz * qz
        radial = -mass * inv3 - 2.5 * rqr * inv7
        sums[0] += rx * radial + qx * inv5
        sums[1] += ry * radial + qy * inv5
        sums[2] += rz * radial + qz * inv5
    lane = lax.broadcasted_iota(I32, (1, LEAF), 1)
    grav = 1.0 / (near_ref.shape[1] * LEAF)
    for c in range(3):
        rows_ref[c] = sums[c] * grav
        for b in range(BLK):
            out_ref[c : c + 1, b * LEAF : (b + 1) * LEAF] = jnp.where(lane < counts_ref[b], rows_ref[c, b : b + 1, :], 0.0)


def near_scratch(sets):
    return [
        pltpu.VMEM((sets * BODY + 8, 128), F32),
        pltpu.VMEM((LEAF, BLK), F32),
        pltpu.VMEM((LEAF, BLK), F32),
        pltpu.VMEM((LEAF, BLK), F32),
        pltpu.VMEM((3, BLK * LEAF, 128), F32),
        pltpu.SMEM((BLK, 24), I32),
    ]


def params(mib):
    return pltpu.CompilerParams(vmem_limit_bytes=mib << 20)


def cost(flops):
    return pl.CostEstimate(flops=flops, bytes_accessed=1 << 18, transcendentals=0)


def exchange(payload, axis, flip):
    return lax.ppermute(payload, axis, [(i, flip(i)) for i in range(lax.axis_size(axis))])


def step(positions, masses, counts, near_list, far_list):
    wide_bits = lax.axis_size("wide").bit_length() - 1
    shape = (BODY + 8, 128)
    own = pl.pallas_call(
        pack_kernel,
        out_shape=jax.ShapeDtypeStruct(shape, F32),
        in_specs=[HBM, HBM, HBM],
        out_specs=VMEM,
        scratch_shapes=[
            pltpu.SMEM(counts.shape, I32),
            pltpu.VMEM(positions.shape, F32),
            pltpu.VMEM((16, 128), F32),
            pltpu.SemaphoreType.DMA((3,)),
        ],
        compiler_params=params(4),
        name="pack",
    )(*(pltpu.with_memory_space_constraint(a, pltpu.HBM) for a in (counts, positions, masses.reshape(16, 128))))
    wide = [exchange(own, "wide", lambda i, bit=bit: i ^ (1 << bit)) for bit in range(wide_bits)]
    message = pl.pallas_call(
        join_kernel,
        out_shape=jax.ShapeDtypeStruct((4, *shape), F32),
        in_specs=[VMEM] * (1 + wide_bits),
        out_specs=VMEM,
        compiler_params=params(4),
        name="join",
    )(own, *wide)
    y_groups = [[z + 4 * y for y in range(4)] for z in range(4)]
    y_all = lax.all_to_all(message, "oct", 0, 0, axis_index_groups=y_groups)
    cells = y_all[:, BODY : BODY + 4, :].reshape(16, 128)
    mine = jnp.concatenate([own[:BODY], cells], axis=0)
    z_one = exchange(mine, "oct", lambda i: i ^ 1)
    partial = jax.ShapeDtypeStruct((3, BLK, LEAF), F32)
    first = pl.pallas_call(
        first_near_kernel,
        out_shape=partial,
        in_specs=[SMEM, SMEM, VMEM] + [VMEM] * wide_bits,
        out_specs=VMEM,
        scratch_shapes=near_scratch(1 + wide_bits),
        compiler_params=params(16),
        cost_estimate=cost(40 << 20),
        name="near_one",
    )(near_list, counts, mine, *wide)
    relay = jnp.concatenate([z_one[:BODY], cells, z_one[BODY:]], axis=0)
    z_two = exchange(relay, "oct", lambda i: (i & ~3) | RELAY[i & 3])
    second = pl.pallas_call(
        second_near_kernel,
        out_shape=partial,
        in_specs=[SMEM, SMEM] + [VMEM] * 4,
        out_specs=VMEM,
        scratch_shapes=near_scratch(3),
        compiler_params=params(16),
        cost_estimate=cost(20 << 20),
        name="near_two",
    )(near_list, counts, mine, relay, y_all, first)
    return pl.pallas_call(
        last_kernel,
        out_shape=jax.ShapeDtypeStruct(positions.shape, F32),
        in_specs=[SMEM, SMEM, SMEM] + [VMEM] * 5,
        out_specs=VMEM,
        scratch_shapes=[
            pltpu.VMEM((64, 128), F32),
            pltpu.VMEM((2, BLK * far_list.shape[1], 128), F32),
            pltpu.VMEM((3, BLK, LEAF), F32),
            *near_scratch(1),
        ],
        compiler_params=params(16),
        cost_estimate=cost(20 << 20),
        name="last",
    )(near_list, far_list, counts, far_list, mine, z_one, z_two, second)


def solution(mesh):
    return jax.shard_map(
        step,
        mesh=mesh,
        in_specs=(
            P(None, ("wide", "oct")),
            P(("wide", "oct")),
            P(("wide", "oct")),
            P(("wide", "oct"), None),
            P(("wide", "oct"), None),
        ),
        out_specs=P(None, ("wide", "oct")),
        check_vma=False,
    )
```

```python
import jax
import jax.numpy as jnp
from jax import lax
from jax.experimental import pallas as pl
from jax.experimental.pallas import tpu as pltpu
from jax.sharding import PartitionSpec as P


near_soft = 0.01
far_soft = 0.25
BLK = 8
LEAF = 256
BODY = BLK * 8
SLOT = 16
F32 = jnp.float32
I32 = jnp.int32
VMEM = pl.BlockSpec(memory_space=pltpu.VMEM)
SMEM = pl.BlockSpec(memory_space=pltpu.SMEM)
HBM = pl.BlockSpec(memory_space=pltpu.HBM)
RELAY = (3, 2, 1, 0)


def planes(ref):
    half = [[ref[pl.ds(h * 4 + c, BLK, stride=8), :] for h in range(2)] for c in range(4)]
    return [jnp.concatenate(pair, axis=1) for pair in half]


def pack_kernel(counts_hbm, pos_hbm, mass_hbm, out_ref, counts_ref, pos_ref, mass_ref, sems):
    copies = [
        pltpu.make_async_copy(src, dst, sems.at[i])
        for i, (src, dst) in enumerate(((pos_hbm, pos_ref), (mass_hbm, mass_ref), (counts_hbm, counts_ref)))
    ]
    for copy in copies:
        copy.start()
    for copy in copies:
        copy.wait()
    lane = lax.broadcasted_iota(I32, (1, 128), 1)
    for b in range(BLK):
        for half in range(2):
            row = b * 8 + half * 4
            at = b * LEAF + half * 128
            for c in range(3):
                out_ref[row + c : row + c + 1, :] = pos_ref[c : c + 1, at : at + 128]
            live = lane + half * 128 < counts_ref[b]
            out_ref[row + 3 : row + 4, :] = jnp.where(live, mass_ref[2 * b + half : 2 * b + half + 1, :], 0.0)
    x, y, z, m = planes(out_ref)

    def total(a):
        return jnp.sum(a, axis=1, keepdims=True)

    mass = total(m)
    cx, cy, cz = total(x * m) / mass, total(y * m) / mass, total(z * m) / mass
    dx, dy, dz = x - cx, y - cy, z - cz
    mx, my, mz = m * dx, m * dy, m * dz
    xx, yy, zz = total(mx * dx), total(my * dy), total(mz * dz)
    trace = xx + yy + zz
    first = [mass, cx, cy, cz, 3.0 * xx - trace, 3.0 * yy - trace, 3.0 * zz - trace, 3.0 * total(mx * dy)]
    last = [3.0 * total(mx * dz), 3.0 * total(my * dz)]
    lanes = lax.broadcasted_iota(I32, (BLK, 128), 1)
    blocks = lax.broadcasted_iota(I32, (BLK, 128), 0)

    def cell_row(columns):
        tile = jnp.zeros((BLK, 128), F32)
        for k, column in enumerate(columns):
            tile = jnp.where(lanes % SLOT == k, column, tile)
        return jnp.sum(jnp.where(lanes // SLOT == blocks, tile, 0.0), axis=0, keepdims=True)

    rows = jnp.where(blocks == 0, cell_row(first), 0.0)
    out_ref[BODY:, :] = jnp.where(blocks == 1, cell_row(last), rows)


def join_kernel(*refs):
    *sets, out_ref = refs
    first = [ref[BODY : BODY + 1, :] for ref in sets]
    last = sum(pltpu.roll(jnp.broadcast_to(ref[BODY + 1 : BODY + 2, :], (8, 128)), 2 * g, 1) if g else jnp.broadcast_to(ref[BODY + 1 : BODY + 2, :], (8, 128)) for g, ref in enumerate(sets))
    at = lax.broadcasted_iota(I32, (8, 128), 0)
    tile = jnp.where(at == 3, last, 0.0)
    for g in range(0, len(sets), 2):
        pair = jnp.broadcast_to(first[g], (8, 128))
        if g + 1 < len(sets):
            pair = pair + pltpu.roll(jnp.broadcast_to(first[g + 1], (8, 128)), 8, 1)
        tile = jnp.where(at == g // 2, pair, tile)
    for k in range(out_ref.shape[0]):
        out_ref[k, :BODY, :] = sets[0][:BODY, :]
        out_ref[k, BODY:, :] = tile


def spread_targets(own, target_ref):
    for c, plane in enumerate(planes(own)[:3]):
        columns = plane.T
        for b in range(BLK):
            target_ref[c, b * LEAF : (b + 1) * LEAF, :] = jnp.broadcast_to(columns[:, b : b + 1], (LEAF, 128))


def near_part(near_ref, counts_ref, target_ref, sums_ref, source_ref, bodies, levels):
    lane8 = lax.broadcasted_iota(I32, (BLK, 128), 1)
    block8 = lax.broadcasted_iota(I32, (BLK, 128), 0)
    masks = []
    for s, body in enumerate(bodies):
        for b in range(BLK):
            source_ref[s * BODY + b * 8 : s * BODY + b * 8 + 8, :] = body(b)
        second = source_ref[pl.ds(s * BODY + 7, BLK, stride=8), :]
        masks.append(jnp.sum(jnp.where((lane8 == 0) & (second > 0.0), jnp.left_shift(1, block8), 0)))
    entries = near_ref.shape[1]

    def run(row, first, count, groups, halves):
        s = [
            [jnp.broadcast_to(source_ref[pl.ds(row + 4 * h + c, 1), :], (8, 128)) for c in range(4)]
            for h in range(halves)
        ]

        def chunk(g, carry):
            start = pl.multiple_of(first + g * (8 * groups), 8)
            for i in range(groups):
                at = pl.ds(start + 8 * i, 8)
                t = [target_ref[c, at, :] for c in range(3)]
                sums = [sums_ref[c, at, :] for c in range(3)]
                for h in range(halves):
                    dx, dy, dz = s[h][0] - t[0], s[h][1] - t[1], s[h][2] - t[2]
                    inv = lax.rsqrt(dx * dx + dy * dy + dz * dz + near_soft)
                    w = s[h][3] * (inv * inv * inv)
                    sums = [sums[0] + dx * w, sums[1] + dy * w, sums[2] + dz * w]
                for c in range(3):
                    sums_ref[c, at, :] = sums[c]
            return carry

        lax.fori_loop(0, (count + 8 * groups - 1) // (8 * groups), chunk, 0)

    def item(k, carry):
        b = k // entries
        code = near_ref[b, k % entries]
        level, slot = code // BLK, code % BLK
        local = jnp.int32(-1)
        mask = jnp.int32(0)
        for s, name in enumerate(levels):
            local = jnp.where(level == name, s, local)
            mask = jnp.where(level == name, masks[s], mask)
        row = local * BODY + slot * 8
        both = jnp.right_shift(mask, slot) % 2 == 1
        first, count = b * LEAF, counts_ref[b]

        @pl.when((local >= 0) & both)
        def _():
            run(row, first, count, 4, 2)

        @pl.when((local >= 0) & jnp.logical_not(both))
        def _():
            run(row, first, count, 8, 1)

        return carry

    lax.fori_loop(0, BLK * entries, item, 0)


def block_of(ref):
    return lambda b: ref[b * 8 : b * 8 + 8, :]


LEVELS_ONE, LEVELS_TWO, LEVELS_THREE, LEVELS_LAST = (0, 5, 6), (7, 8, 9), (1, 3, 4), (2,)


def near_one_kernel(near_ref, counts_ref, own, wide_a, wide_b, sums_ref, target_ref, source_ref):
    spread_targets(own, target_ref)
    sums_ref[...] = jnp.zeros_like(sums_ref)
    bodies = [*map(block_of, (own, wide_a, wide_b))]
    near_part(near_ref, counts_ref, target_ref, sums_ref, source_ref, bodies, LEVELS_ONE)


def near_two_kernel(near_ref, counts_ref, wide_a, wide_b, wide_c, mine, before, target_ref, sums_ref, source_ref):
    spread_targets(mine, target_ref)
    bodies = [*map(block_of, (wide_a, wide_b, wide_c))]
    near_part(near_ref, counts_ref, target_ref, sums_ref, source_ref, bodies, LEVELS_TWO)


def near_three_kernel(near_ref, counts_ref, z_one, y_all, target_ref, before, sums_ref, source_ref):
    y = lax.axis_index("oct") // 4

    def member(flip):
        return lambda b: y_all[y ^ flip, b * 8 : b * 8 + 8, :]

    bodies = [block_of(z_one), member(1), member(2)]
    near_part(near_ref, counts_ref, target_ref, sums_ref, source_ref, bodies, LEVELS_THREE)


def three_parts(a):
    hi = a.astype(jnp.bfloat16)
    rest = a - hi.astype(F32)
    mid = rest.astype(jnp.bfloat16)
    return hi, mid, (rest - mid.astype(F32)).astype(jnp.bfloat16)


def last_kernel(near_ref, far_ref, counts_ref, own, z_one, z_two, target_ref, before, out_ref, sums_ref, table_ref, rows_ref, source_ref):
    near_part(near_ref, counts_ref, target_ref, sums_ref, source_ref, [block_of(z_two)], LEVELS_LAST)
    sums = []
    lane8 = lax.broadcasted_iota(I32, (LEAF, BLK), 1)
    for c in range(3):
        columns = jnp.zeros((LEAF, BLK), F32)
        for b in range(BLK):
            part = jnp.sum(sums_ref[c, b * LEAF : (b + 1) * LEAF, :], axis=1, keepdims=True)
            columns = jnp.where(lane8 == b, part, columns)
        sums.append(columns.T)
    me = lax.axis_index("oct") % 4
    other = 3 - me
    n = z_one.shape[0] - BODY
    for place, rows in (
        (me, own[BODY:, :]),
        (me ^ 1, z_one[BODY:, :]),
        (other, z_two[BODY : BODY + n, :]),
        (other ^ 1, z_two[BODY + n :, :]),
    ):
        table_ref[pl.ds(pl.multiple_of(place * n, n), n), :] = rows
    members = lax.axis_size("oct")
    far_count = far_ref.shape[1]
    picks = BLK * far_count
    lanes = lax.broadcasted_iota(I32, (picks, 128), 1)
    code = jnp.concatenate([jnp.broadcast_to(far_ref[:, v : v + 1], (BLK, 128)) for v in range(far_count)], axis=0)
    group, member, slot = code // (BLK * members), code // BLK % members, code % BLK
    row = member % 4 * n + member // 4 * 4
    table = jnp.concatenate(three_parts(table_ref[...]), axis=1)
    folded = jnp.zeros((picks, 128), F32)
    lhs, rhs = [], []
    fold_from = lax.broadcasted_iota(I32, (128, 128), 0)
    fold_to = lax.broadcasted_iota(I32, (128, 128), 1)
    for at_row, low, width, base in (
        (row + group // 2, slot * SLOT + group % 2 * 8, 8, 0),
        (row + 3, slot * SLOT + group * 2, 2, 8),
    ):
        hot = (lanes == at_row)[:, : table_ref.shape[0]].astype(F32).astype(jnp.bfloat16)
        rows = jnp.dot(hot, table, preferred_element_type=F32)
        keep = (lanes >= low) & (lanes < low + width)
        fold = (fold_from % width + base == fold_to).astype(F32).astype(jnp.bfloat16)
        for part in range(3):
            chosen = jnp.where(keep, rows[:, part * 128 : (part + 1) * 128], 0.0)
            lhs.append(chosen.astype(jnp.bfloat16))
            rhs.append(fold)
    folded = jnp.dot(jnp.concatenate(lhs, axis=1), jnp.concatenate(rhs, axis=0), preferred_element_type=F32)
    x, y, z, _ = planes(own)
    for v in range(far_count):
        tile = folded[v * BLK : (v + 1) * BLK, :]
        mass, cx, cy, cz, xx, yy, zz, xy, xz, yz = (tile[:, k : k + 1] for k in range(10))
        rx, ry, rz = x - cx, y - cy, z - cz
        inv = lax.rsqrt(rx * rx + ry * ry + rz * rz + far_soft)
        inv2 = inv * inv
        inv3 = inv * inv2
        inv5 = inv3 * inv2
        inv7 = inv5 * inv2
        qx = xx * rx + xy * ry + xz * rz
        qy = xy * rx + yy * ry + yz * rz
        qz = xz * rx + yz * ry + zz * rz
        rqr = rx * qx + ry * qy + rz * qz
        radial = -mass * inv3 - 2.5 * rqr * inv7
        sums[0] += rx * radial + qx * inv5
        sums[1] += ry * radial + qy * inv5
        sums[2] += rz * radial + qz * inv5
    lane = lax.broadcasted_iota(I32, (1, LEAF), 1)
    grav = 1.0 / (near_ref.shape[1] * LEAF)
    for c in range(3):
        rows_ref[c] = sums[c] * grav
        for b in range(BLK):
            out_ref[c : c + 1, b * LEAF : (b + 1) * LEAF] = jnp.where(lane < counts_ref[b], rows_ref[c, b : b + 1, :], 0.0)


def sources(sets):
    return pltpu.VMEM((sets * BODY, 128), F32)


def params(mib):
    return pltpu.CompilerParams(vmem_limit_bytes=mib << 20)


def cost(flops):
    return pl.CostEstimate(flops=flops, bytes_accessed=1 << 18, transcendentals=0)


def mine_kernel(own, y_all, out_ref):
    out_ref[:BODY, :] = own[:BODY, :]
    for y in range(4):
        out_ref[BODY + 4 * y : BODY + 4 * y + 4, :] = y_all[y, BODY : BODY + 4, :]


def relay_kernel(mine, z_one, out_ref):
    n = z_one.shape[0] - BODY
    out_ref[:BODY, :] = z_one[:BODY, :]
    out_ref[BODY : BODY + n, :] = mine[BODY:, :]
    out_ref[BODY + n :, :] = z_one[BODY:, :]


def small_call(kernel, rows, *operands):
    return pl.pallas_call(
        kernel,
        out_shape=jax.ShapeDtypeStruct((rows, 128), F32),
        in_specs=[VMEM] * len(operands),
        out_specs=VMEM,
        compiler_params=params(2),
    )(*operands)


def exchange(payload, axis, flip):
    return lax.ppermute(payload, axis, [(i, flip(i)) for i in range(lax.axis_size(axis))])


def step(positions, masses, counts, near_list, far_list):
    wide_bits = lax.axis_size("wide").bit_length() - 1
    shape = (BODY + 8, 128)
    own = pl.pallas_call(
        pack_kernel,
        out_shape=jax.ShapeDtypeStruct(shape, F32),
        in_specs=[HBM, HBM, HBM],
        out_specs=VMEM,
        scratch_shapes=[
            pltpu.SMEM(counts.shape, I32),
            pltpu.VMEM(positions.shape, F32),
            pltpu.VMEM((16, 128), F32),
            pltpu.SemaphoreType.DMA((3,)),
        ],
        compiler_params=params(4),
        name="pack",
    )(*(pltpu.with_memory_space_constraint(a, pltpu.HBM) for a in (counts, positions, masses.reshape(16, 128))))
    wide = [exchange(own, "wide", lambda i, bit=bit: i ^ (1 << bit)) for bit in range(wide_bits)]
    message = pl.pallas_call(
        join_kernel,
        out_shape=jax.ShapeDtypeStruct((4, *shape), F32),
        in_specs=[VMEM] * (1 + wide_bits),
        out_specs=VMEM,
        compiler_params=params(4),
        name="join",
    )(own, *wide)
    y_groups = [[z + 4 * y for y in range(4)] for z in range(4)]
    y_all = lax.all_to_all(message, "oct", 0, 0, axis_index_groups=y_groups)
    state = jax.ShapeDtypeStruct((3, BLK * LEAF, 128), F32)
    sums = pl.pallas_call(
        near_one_kernel,
        out_shape=state,
        in_specs=[SMEM, SMEM] + [VMEM] * 3,
        out_specs=VMEM,
        scratch_shapes=[pltpu.VMEM(state.shape, F32), sources(3)],
        compiler_params=params(8),
        cost_estimate=cost(20 << 20),
        name="near_one",
    )(near_list, counts, own, wide[0], wide[1])
    mine = small_call(mine_kernel, BODY + 16, own, y_all)
    z_one = exchange(mine, "oct", lambda i: i ^ 1)
    targets, sums = pl.pallas_call(
        near_two_kernel,
        out_shape=[state, state],
        in_specs=[SMEM, SMEM] + [VMEM] * 5,
        out_specs=[VMEM, VMEM],
        scratch_shapes=[sources(3)],
        input_output_aliases={6: 1},
        compiler_params=params(8),
        cost_estimate=cost(20 << 20),
        name="near_two",
    )(near_list, counts, *wide[2:], mine, sums)
    relay = small_call(relay_kernel, BODY + 32, mine, z_one)
    z_two = exchange(relay, "oct", lambda i: (i & ~3) | RELAY[i & 3])
    sums = pl.pallas_call(
        near_three_kernel,
        out_shape=state,
        in_specs=[SMEM, SMEM] + [VMEM] * 4,
        out_specs=VMEM,
        scratch_shapes=[sources(3)],
        input_output_aliases={5: 0},
        compiler_params=params(8),
        cost_estimate=cost(20 << 20),
        name="near_three",
    )(near_list, counts, relay, y_all, targets, sums)
    return pl.pallas_call(
        last_kernel,
        out_shape=[jax.ShapeDtypeStruct(positions.shape, F32), state],
        in_specs=[SMEM, VMEM, SMEM] + [VMEM] * 5,
        out_specs=[VMEM, VMEM],
        scratch_shapes=[
            pltpu.VMEM((64, 128), F32),
            pltpu.VMEM((3, BLK, LEAF), F32),
            sources(1),
        ],
        input_output_aliases={7: 1},
        compiler_params=params(8),
        cost_estimate=cost(20 << 20),
        name="last",
    )(near_list, far_list, counts, mine, z_one, z_two, targets, sums)[0]


def solution(mesh):
    return jax.shard_map(
        step,
        mesh=mesh,
        in_specs=(
            P(None, ("wide", "oct")),
            P(("wide", "oct")),
            P(("wide", "oct")),
            P(("wide", "oct"), None),
            P(("wide", "oct"), None),
        ),
        out_specs=P(None, ("wide", "oct")),
        check_vma=False,
    )
```

```python
import functools

import jax
import jax.numpy as jnp
from jax import lax
from jax.experimental import pallas as pl
from jax.experimental.pallas import tpu as pltpu
from jax.sharding import PartitionSpec as P


near_soft = 0.01
far_soft = 0.25
BLK = 8
LEAF = 256
BODY = BLK * 8
GROUPS = 8
SLOT = 16
F32 = jnp.float32
I32 = jnp.int32
VMEM = pl.BlockSpec(memory_space=pltpu.VMEM)
SMEM = pl.BlockSpec(memory_space=pltpu.SMEM)
HBM = pl.BlockSpec(memory_space=pltpu.HBM)
RELAY = (3, 2, 1, 0)
COUNT = 16
STAGES = ((0, 5, 6), (7, 8, 9), (1, 3, 4), (2,))


def planes(ref):
    half = [[ref[pl.ds(h * 4 + c, BLK, stride=8), :] for h in range(2)] for c in range(4)]
    return [jnp.concatenate(pair, axis=1) for pair in half]


def pack_kernel(counts_hbm, pos_hbm, mass_hbm, near_hbm, out_ref, control_ref, counts_ref, pos_ref, mass_ref, near_ref, sems):
    moves = ((pos_hbm, pos_ref), (mass_hbm, mass_ref), (counts_hbm, counts_ref), (near_hbm, near_ref))
    copies = [pltpu.make_async_copy(src, dst, sems.at[i]) for i, (src, dst) in enumerate(moves)]
    for copy in copies:
        copy.start()
    for copy in copies:
        copy.wait()
    lane = lax.broadcasted_iota(I32, (1, 128), 1)
    for b in range(BLK):
        for half in range(2):
            row = b * 8 + half * 4
            at = b * LEAF + half * 128
            for c in range(3):
                out_ref[row + c : row + c + 1, :] = pos_ref[c : c + 1, at : at + 128]
            live = lane + half * 128 < counts_ref[b]
            out_ref[row + 3 : row + 4, :] = jnp.where(live, mass_ref[2 * b + half : 2 * b + half + 1, :], 0.0)
    x, y, z, m = planes(out_ref)

    def total(a):
        return jnp.sum(a, axis=1, keepdims=True)

    mass = total(m)
    cx, cy, cz = total(x * m) / mass, total(y * m) / mass, total(z * m) / mass
    dx, dy, dz = x - cx, y - cy, z - cz
    mx, my, mz = m * dx, m * dy, m * dz
    xx, yy, zz = total(mx * dx), total(my * dy), total(mz * dz)
    trace = xx + yy + zz
    first = [mass, cx, cy, cz, 3.0 * xx - trace, 3.0 * yy - trace, 3.0 * zz - trace, 3.0 * total(mx * dy)]
    last = [3.0 * total(mx * dz), 3.0 * total(my * dz)]
    lanes = lax.broadcasted_iota(I32, (BLK, 128), 1)
    blocks = lax.broadcasted_iota(I32, (BLK, 128), 0)

    def cell_row(columns):
        tile = jnp.zeros((BLK, 128), F32)
        for k, column in enumerate(columns):
            tile = jnp.where(lanes % SLOT == k, column, tile)
        return jnp.sum(jnp.where(lanes // SLOT == blocks, tile, 0.0), axis=0, keepdims=True)

    rows = jnp.where(blocks == 0, cell_row(first), 0.0)
    out_ref[BODY:, :] = jnp.where(blocks == 1, cell_row(last), rows)
    code = near_ref[...]
    level = code // BLK
    entry = jnp.zeros_like(code)
    for stage, names in enumerate(STAGES):
        for place, name in enumerate(names):
            entry = jnp.where(level == name, stage * 4096 + place * BODY, entry)
    entry = entry + code % BLK * 8
    control = jnp.concatenate([entry, jnp.zeros((BLK, 128 - entry.shape[1]), I32)], axis=1)
    count = jnp.zeros((BLK, 128), I32)
    for b in range(BLK):
        count = jnp.where(blocks == b, counts_ref[b], count)
    control_ref[...] = jnp.where(lanes == COUNT, count, control)


def join_kernel(*refs):
    *sets, out_ref = refs
    first = [ref[BODY : BODY + 1, :] for ref in sets]
    last = sum(pltpu.roll(jnp.broadcast_to(ref[BODY + 1 : BODY + 2, :], (8, 128)), 2 * g, 1) if g else jnp.broadcast_to(ref[BODY + 1 : BODY + 2, :], (8, 128)) for g, ref in enumerate(sets))
    at = lax.broadcasted_iota(I32, (8, 128), 0)
    tile = jnp.where(at == 3, last, 0.0)
    for g in range(0, len(sets), 2):
        pair = jnp.broadcast_to(first[g], (8, 128))
        if g + 1 < len(sets):
            pair = pair + pltpu.roll(jnp.broadcast_to(first[g + 1], (8, 128)), 8, 1)
        tile = jnp.where(at == g // 2, pair, tile)
    for k in range(out_ref.shape[0]):
        out_ref[k, :BODY, :] = sets[0][:BODY, :]
        out_ref[k, BODY:, :] = tile


def spread_targets(own, target_ref):
    k = lax.broadcasted_iota(I32, (3 * BLK, BLK * 128), 0)
    n = lax.broadcasted_iota(I32, (3 * BLK, BLK * 128), 1)
    ones = (k % BLK == n // 128).astype(F32).astype(jnp.bfloat16)
    for c, plane in enumerate(planes(own)[:3]):
        parts = jnp.concatenate([part.astype(F32) for part in three_parts(plane)], axis=0).astype(jnp.bfloat16)
        spread = lax.dot_general(parts, ones, (((0,), (0,)), ((), ())), preferred_element_type=F32)
        for b in range(BLK):
            target_ref[c, b * LEAF : (b + 1) * LEAF, :] = spread[:, b * 128 : (b + 1) * 128]


def near_part(control_ref, target_ref, sums_ref, source_ref, masks_ref, bodies, stage, entries):
    lane8 = lax.broadcasted_iota(I32, (BLK, 128), 1)
    block8 = lax.broadcasted_iota(I32, (BLK, 128), 0)
    for s, body in enumerate(bodies):
        for b in range(BLK):
            source_ref[s * BODY + b * 8 : s * BODY + b * 8 + 8, :] = body(b)
    for s in range(len(bodies)):
        second = source_ref[pl.ds(s * BODY + 7, BLK, stride=8), :]
        masks_ref[s] = jnp.sum(jnp.where((lane8 == 0) & (second > 0.0), jnp.left_shift(1, block8), 0))

    def run(row, first, count, halves):
        s = [
            [jnp.broadcast_to(source_ref[pl.ds(row + 4 * h + c, 1), :], (8, 128)) for c in range(4)]
            for h in range(halves)
        ]

        def chunk(g, carry):
            start = pl.multiple_of(first + g * (8 * GROUPS), 8)
            for i in range(GROUPS):
                at = pl.ds(start + 8 * i, 8)
                t = [target_ref[c, at, :] for c in range(3)]
                sums = [sums_ref[c, at, :] for c in range(3)]
                for h in range(halves):
                    dx, dy, dz = s[h][0] - t[0], s[h][1] - t[1], s[h][2] - t[2]
                    inv = lax.rsqrt(dx * dx + dy * dy + dz * dz + near_soft)
                    w = s[h][3] * (inv * inv * inv)
                    sums = [sums[0] + dx * w, sums[1] + dy * w, sums[2] + dz * w]
                for c in range(3):
                    sums_ref[c, at, :] = sums[c]
            return carry

        lax.fori_loop(0, (count + 8 * GROUPS - 1) // (8 * GROUPS), chunk, 0)

    def block(b, carry):
        first, count = b * LEAF, control_ref[b, COUNT]
        for v in range(entries):
            entry = control_ref[b, v]
            row = entry % 4096
            both = jnp.right_shift(masks_ref[row // BODY], row // 8 % BLK) % 2

            @pl.when(entry // 4096 == stage)
            def _():
                @pl.when(both == 1)
                def _():
                    run(row, first, count, 2)

                @pl.when(both == 0)
                def _():
                    run(row, first, count, 1)

        return carry

    lax.fori_loop(0, BLK, block, 0)


def block_of(ref):
    return lambda b: ref[b * 8 : b * 8 + 8, :]


def near_one_kernel(control_ref, own, wide_a, wide_b, sums_ref, target_ref, source_ref, masks_ref, *, entries):
    spread_targets(own, target_ref)
    sums_ref[...] = jnp.zeros_like(sums_ref)
    bodies = [*map(block_of, (own, wide_a, wide_b))]
    near_part(control_ref, target_ref, sums_ref, source_ref, masks_ref, bodies, 0, entries)


def near_two_kernel(control_ref, wide_a, wide_b, wide_c, mine, before, target_ref, sums_ref, source_ref, masks_ref, *, entries):
    spread_targets(mine, target_ref)
    bodies = [*map(block_of, (wide_a, wide_b, wide_c))]
    near_part(control_ref, target_ref, sums_ref, source_ref, masks_ref, bodies, 1, entries)


def near_three_kernel(control_ref, z_one, y_all, target_ref, before, sums_ref, source_ref, masks_ref, *, entries):
    y = lax.axis_index("oct") // 4

    def member(flip):
        return lambda b: y_all[y ^ flip, b * 8 : b * 8 + 8, :]

    bodies = [block_of(z_one), member(1), member(2)]
    near_part(control_ref, target_ref, sums_ref, source_ref, masks_ref, bodies, 2, entries)


def three_parts(a):
    hi = a.astype(jnp.bfloat16)
    rest = a - hi.astype(F32)
    mid = rest.astype(jnp.bfloat16)
    return hi, mid, (rest - mid.astype(F32)).astype(jnp.bfloat16)


def last_kernel(control_ref, far_ref, own, z_one, z_two, target_ref, before, out_ref, sums_ref, table_ref, rows_ref, source_ref, masks_ref, *, entries):
    near_part(control_ref, target_ref, sums_ref, source_ref, masks_ref, [block_of(z_two)], 3, entries)
    sums = []
    lane8 = lax.broadcasted_iota(I32, (LEAF, BLK), 1)
    for c in range(3):
        columns = jnp.zeros((LEAF, BLK), F32)
        for b in range(BLK):
            part = jnp.sum(sums_ref[c, b * LEAF : (b + 1) * LEAF, :], axis=1, keepdims=True)
            columns = jnp.where(lane8 == b, part, columns)
        sums.append(columns.T)
    me = lax.axis_index("oct") % 4
    other = 3 - me
    n = z_one.shape[0] - BODY
    for place, rows in (
        (me, own[BODY:, :]),
        (me ^ 1, z_one[BODY:, :]),
        (other, z_two[BODY : BODY + n, :]),
        (other ^ 1, z_two[BODY + n :, :]),
    ):
        table_ref[pl.ds(pl.multiple_of(place * n, n), n), :] = rows
    members = lax.axis_size("oct")
    far_count = far_ref.shape[1]
    picks = BLK * far_count
    lanes = lax.broadcasted_iota(I32, (picks, 128), 1)
    code = jnp.concatenate([jnp.broadcast_to(far_ref[:, v : v + 1], (BLK, 128)) for v in range(far_count)], axis=0)
    group, member, slot = code // (BLK * members), code // BLK % members, code % BLK
    row = member % 4 * n + member // 4 * 4
    table = jnp.concatenate(three_parts(table_ref[...]), axis=1)
    folded = jnp.zeros((picks, 128), F32)
    lhs, rhs = [], []
    fold_from = lax.broadcasted_iota(I32, (128, 128), 0)
    fold_to = lax.broadcasted_iota(I32, (128, 128), 1)
    for at_row, low, width, base in (
        (row + group // 2, slot * SLOT + group % 2 * 8, 8, 0),
        (row + 3, slot * SLOT + group * 2, 2, 8),
    ):
        hot = (lanes == at_row)[:, : table_ref.shape[0]].astype(F32).astype(jnp.bfloat16)
        rows = jnp.dot(hot, table, preferred_element_type=F32)
        keep = (lanes >= low) & (lanes < low + width)
        fold = (fold_from % width + base == fold_to).astype(F32).astype(jnp.bfloat16)
        for part in range(3):
            chosen = jnp.where(keep, rows[:, part * 128 : (part + 1) * 128], 0.0)
            lhs.append(chosen.astype(jnp.bfloat16))
            rhs.append(fold)
    folded = jnp.dot(jnp.concatenate(lhs, axis=1), jnp.concatenate(rhs, axis=0), preferred_element_type=F32)
    x, y, z, _ = planes(own)
    for v in range(far_count):
        tile = folded[v * BLK : (v + 1) * BLK, :]
        mass, cx, cy, cz, xx, yy, zz, xy, xz, yz = (tile[:, k : k + 1] for k in range(10))
        rx, ry, rz = x - cx, y - cy, z - cz
        inv = lax.rsqrt(rx * rx + ry * ry + rz * rz + far_soft)
        inv2 = inv * inv
        inv3 = inv * inv2
        inv5 = inv3 * inv2
        inv7 = inv5 * inv2
        qx = xx * rx + xy * ry + xz * rz
        qy = xy * rx + yy * ry + yz * rz
        qz = xz * rx + yz * ry + zz * rz
        rqr = rx * qx + ry * qy + rz * qz
        radial = -mass * inv3 - 2.5 * rqr * inv7
        sums[0] += rx * radial + qx * inv5
        sums[1] += ry * radial + qy * inv5
        sums[2] += rz * radial + qz * inv5
    lane = lax.broadcasted_iota(I32, (1, LEAF), 1)
    grav = 1.0 / (entries * LEAF)
    for c in range(3):
        rows_ref[c] = sums[c] * grav
        for b in range(BLK):
            out_ref[c : c + 1, b * LEAF : (b + 1) * LEAF] = jnp.where(lane < control_ref[b, COUNT], rows_ref[c, b : b + 1, :], 0.0)


def sources(sets):
    return [pltpu.VMEM((sets * BODY, 128), F32), pltpu.SMEM((4,), I32)]


def params(mib):
    return pltpu.CompilerParams(vmem_limit_bytes=mib << 20)


def cost(flops):
    return pl.CostEstimate(flops=flops, bytes_accessed=1 << 18, transcendentals=0)


def mine_kernel(own, y_all, out_ref):
    out_ref[:BODY, :] = own[:BODY, :]
    for y in range(4):
        out_ref[BODY + 4 * y : BODY + 4 * y + 4, :] = y_all[y, BODY : BODY + 4, :]


def relay_kernel(mine, z_one, out_ref):
    n = z_one.shape[0] - BODY
    out_ref[:BODY, :] = z_one[:BODY, :]
    out_ref[BODY : BODY + n, :] = mine[BODY:, :]
    out_ref[BODY + n :, :] = z_one[BODY:, :]


def small_call(kernel, rows, *operands):
    return pl.pallas_call(
        kernel,
        out_shape=jax.ShapeDtypeStruct((rows, 128), F32),
        in_specs=[VMEM] * len(operands),
        out_specs=VMEM,
        compiler_params=params(2),
    )(*operands)


def exchange(payload, axis, flip):
    return lax.ppermute(payload, axis, [(i, flip(i)) for i in range(lax.axis_size(axis))])


def step(positions, masses, counts, near_list, far_list):
    wide_bits = lax.axis_size("wide").bit_length() - 1
    shape = (BODY + 8, 128)
    entries = near_list.shape[1]
    own, control = pl.pallas_call(
        pack_kernel,
        out_shape=[jax.ShapeDtypeStruct(shape, F32), jax.ShapeDtypeStruct((BLK, 128), I32)],
        in_specs=[HBM] * 4,
        out_specs=[VMEM, VMEM],
        scratch_shapes=[
            pltpu.SMEM(counts.shape, I32),
            pltpu.VMEM(positions.shape, F32),
            pltpu.VMEM((16, 128), F32),
            pltpu.VMEM(near_list.shape, I32),
            pltpu.SemaphoreType.DMA((4,)),
        ],
        compiler_params=params(4),
        name="pack",
    )(*(pltpu.with_memory_space_constraint(a, pltpu.HBM) for a in (counts, positions, masses.reshape(16, 128), near_list)))
    wide = []
    for bit in range(wide_bits):
        wide.append(exchange(own, "wide", lambda i, bit=bit: i ^ (1 << bit)))
    message = pl.pallas_call(
        join_kernel,
        out_shape=jax.ShapeDtypeStruct((4, *shape), F32),
        in_specs=[VMEM] * (1 + wide_bits),
        out_specs=VMEM,
        compiler_params=params(4),
        name="join",
    )(own, *wide)
    y_groups = [[z + 4 * y for y in range(4)] for z in range(4)]
    y_all = lax.all_to_all(message, "oct", 0, 0, axis_index_groups=y_groups)
    state = jax.ShapeDtypeStruct((3, BLK * LEAF, 128), F32)
    sums = pl.pallas_call(
        functools.partial(near_one_kernel, entries=entries),
        out_shape=state,
        in_specs=[SMEM] + [VMEM] * 3,
        out_specs=VMEM,
        scratch_shapes=[pltpu.VMEM(state.shape, F32), *sources(3)],
        compiler_params=params(8),
        cost_estimate=cost(20 << 20),
        name="near_one",
    )(control, own, wide[0], wide[1])
    mine = small_call(mine_kernel, BODY + 16, own, y_all)
    z_one = exchange(mine, "oct", lambda i: i ^ 1)
    targets, sums = pl.pallas_call(
        functools.partial(near_two_kernel, entries=entries),
        out_shape=[state, state],
        in_specs=[SMEM] + [VMEM] * 5,
        out_specs=[VMEM, VMEM],
        scratch_shapes=sources(3),
        input_output_aliases={5: 1},
        compiler_params=params(8),
        cost_estimate=cost(20 << 20),
        name="near_two",
    )(control, *wide[2:], mine, sums)
    relay = small_call(relay_kernel, BODY + 32, mine, z_one)
    z_two = exchange(relay, "oct", lambda i: (i & ~3) | RELAY[i & 3])
    sums = pl.pallas_call(
        functools.partial(near_three_kernel, entries=entries),
        out_shape=state,
        in_specs=[SMEM] + [VMEM] * 4,
        out_specs=VMEM,
        scratch_shapes=sources(3),
        input_output_aliases={4: 0},
        compiler_params=params(8),
        cost_estimate=cost(20 << 20),
        name="near_three",
    )(control, relay, y_all, targets, sums)
    return pl.pallas_call(
        functools.partial(last_kernel, entries=entries),
        out_shape=[jax.ShapeDtypeStruct(positions.shape, F32), state],
        in_specs=[SMEM] + [VMEM] * 6,
        out_specs=[VMEM, VMEM],
        scratch_shapes=[
            pltpu.VMEM((64, 128), F32),
            pltpu.VMEM((3, BLK, LEAF), F32),
            *sources(1),
        ],
        input_output_aliases={6: 1},
        compiler_params=params(8),
        cost_estimate=cost(20 << 20),
        name="last",
    )(control, far_list, mine, z_one, z_two, targets, sums)[0]


def solution(mesh):
    return jax.shard_map(
        step,
        mesh=mesh,
        in_specs=(
            P(None, ("wide", "oct")),
            P(("wide", "oct")),
            P(("wide", "oct")),
            P(("wide", "oct"), None),
            P(("wide", "oct"), None),
        ),
        out_specs=P(None, ("wide", "oct")),
        check_vma=False,
    )
```

```python
import functools

import jax
import jax.numpy as jnp
from jax import lax
from jax.experimental import pallas as pl
from jax.experimental.pallas import tpu as pltpu
from jax.sharding import PartitionSpec as P


near_soft = 0.01
far_soft = 0.25
BLK = 8
LEAF = 256
BODY = BLK * 8
GROUPS = 8
SLOT = 16
F32 = jnp.float32
I32 = jnp.int32
VMEM = pl.BlockSpec(memory_space=pltpu.VMEM)
SMEM = pl.BlockSpec(memory_space=pltpu.SMEM)
HBM = pl.BlockSpec(memory_space=pltpu.HBM)
RELAY = (3, 2, 1, 0)
COUNT = 127
ITEMS = 64
STAGES = ((0, 5, 6), (7, 8, 9), (1, 3, 4), (2,))


def planes(ref):
    half = [[ref[pl.ds(h * 4 + c, BLK, stride=8), :] for h in range(2)] for c in range(4)]
    return [jnp.concatenate(pair, axis=1) for pair in half]


def pack_kernel(counts_hbm, pos_hbm, mass_hbm, near_hbm, out_ref, control_ref, counts_ref, pos_ref, mass_ref, near_ref, sems):
    moves = ((pos_hbm, pos_ref), (mass_hbm, mass_ref), (counts_hbm, counts_ref), (near_hbm, near_ref))
    copies = [pltpu.make_async_copy(src, dst, sems.at[i]) for i, (src, dst) in enumerate(moves)]
    for copy in copies:
        copy.start()
    for copy in copies:
        copy.wait()
    lane = lax.broadcasted_iota(I32, (1, 128), 1)
    for b in range(BLK):
        for half in range(2):
            row = b * 8 + half * 4
            at = b * LEAF + half * 128
            for c in range(3):
                out_ref[row + c : row + c + 1, :] = pos_ref[c : c + 1, at : at + 128]
            live = lane + half * 128 < counts_ref[b]
            out_ref[row + 3 : row + 4, :] = jnp.where(live, mass_ref[2 * b + half : 2 * b + half + 1, :], 0.0)
    x, y, z, m = planes(out_ref)

    def total(a):
        return jnp.sum(a, axis=1, keepdims=True)

    mass = total(m)
    cx, cy, cz = total(x * m) / mass, total(y * m) / mass, total(z * m) / mass
    dx, dy, dz = x - cx, y - cy, z - cz
    mx, my, mz = m * dx, m * dy, m * dz
    xx, yy, zz = total(mx * dx), total(my * dy), total(mz * dz)
    trace = xx + yy + zz
    first = [mass, cx, cy, cz, 3.0 * xx - trace, 3.0 * yy - trace, 3.0 * zz - trace, 3.0 * total(mx * dy)]
    last = [3.0 * total(mx * dz), 3.0 * total(my * dz)]
    lanes = lax.broadcasted_iota(I32, (BLK, 128), 1)
    blocks = lax.broadcasted_iota(I32, (BLK, 128), 0)

    def cell_row(columns):
        tile = jnp.zeros((BLK, 128), F32)
        for k, column in enumerate(columns):
            tile = jnp.where(lanes % SLOT == k, column, tile)
        return jnp.sum(jnp.where(lanes // SLOT == blocks, tile, 0.0), axis=0, keepdims=True)

    rows = jnp.where(blocks == 0, cell_row(first), 0.0)
    out_ref[BODY:, :] = jnp.where(blocks == 1, cell_row(last), rows)
    code = near_ref[...]
    entries = code.shape[1]
    stage = jnp.zeros_like(code)
    value = lax.broadcasted_iota(I32, code.shape, 0) * 32 + code % BLK
    for number, names in enumerate(STAGES):
        for place, name in enumerate(names):
            stage = jnp.where(code // BLK == name, number, stage)
            value = value + jnp.where(code // BLK == name, place * BLK, 0)

    def column(a):
        return jnp.concatenate([jnp.broadcast_to(a[:, v : v + 1], (BLK, 128)) for v in range(entries)], axis=0).astype(F32)

    stages = column(stage)
    items = BLK * entries
    down = lax.broadcasted_iota(I32, (items, 128), 0).astype(F32)
    across = lax.broadcasted_iota(I32, (items, 128), 1).astype(F32)
    key = stages * items + down
    rank = jnp.sum((key.T[:items, :] < key[:, :items]).astype(F32), axis=1, keepdims=True)
    sorted_items = jnp.where(rank == across, column(value), 0.0)
    starts = (stages < across - ITEMS).astype(F32)
    row = jnp.sum(jnp.where(across < ITEMS, sorted_items, starts), axis=0, keepdims=True).astype(I32)
    control = jnp.where(blocks == 0, row, 0)
    for b in range(BLK):
        control = jnp.where((blocks == b) & (lanes == COUNT), counts_ref[b], control)
    control_ref[...] = control


def join_kernel(*refs):
    *sets, out_ref = refs
    first = [ref[BODY : BODY + 1, :] for ref in sets]
    last = sum(pltpu.roll(jnp.broadcast_to(ref[BODY + 1 : BODY + 2, :], (8, 128)), 2 * g, 1) if g else jnp.broadcast_to(ref[BODY + 1 : BODY + 2, :], (8, 128)) for g, ref in enumerate(sets))
    at = lax.broadcasted_iota(I32, (8, 128), 0)
    tile = jnp.where(at == 3, last, 0.0)
    for g in range(0, len(sets), 2):
        pair = jnp.broadcast_to(first[g], (8, 128))
        if g + 1 < len(sets):
            pair = pair + pltpu.roll(jnp.broadcast_to(first[g + 1], (8, 128)), 8, 1)
        tile = jnp.where(at == g // 2, pair, tile)
    for k in range(out_ref.shape[0]):
        out_ref[k, :BODY, :] = sets[0][:BODY, :]
        out_ref[k, BODY:, :] = tile


def spread_targets(own, target_ref):
    k = lax.broadcasted_iota(I32, (3 * BLK, BLK * 128), 0)
    n = lax.broadcasted_iota(I32, (3 * BLK, BLK * 128), 1)
    ones = (k % BLK == n // 128).astype(F32).astype(jnp.bfloat16)
    for c, plane in enumerate(planes(own)[:3]):
        parts = jnp.concatenate([part.astype(F32) for part in three_parts(plane)], axis=0).astype(jnp.bfloat16)
        spread = lax.dot_general(parts, ones, (((0,), (0,)), ((), ())), preferred_element_type=F32)
        for b in range(BLK):
            target_ref[c, b * LEAF : (b + 1) * LEAF, :] = spread[:, b * 128 : (b + 1) * 128]


def near_part(control_ref, target_ref, sums_ref, source_ref, masks_ref, bodies, stage):
    lane8 = lax.broadcasted_iota(I32, (BLK, 128), 1)
    block8 = lax.broadcasted_iota(I32, (BLK, 128), 0)
    for s, body in enumerate(bodies):
        for b in range(BLK):
            source_ref[s * BODY + b * 8 : s * BODY + b * 8 + 8, :] = body(b)
    for s in range(len(bodies)):
        second = source_ref[pl.ds(s * BODY + 7, BLK, stride=8), :]
        masks_ref[s] = jnp.sum(jnp.where((lane8 == 0) & (second > 0.0), jnp.left_shift(1, block8), 0))

    def run(row, first, count, halves):
        s = [
            [jnp.broadcast_to(source_ref[pl.ds(row + 4 * h + c, 1), :], (8, 128)) for c in range(4)]
            for h in range(halves)
        ]

        def chunk(g, carry):
            start = pl.multiple_of(first + g * (8 * GROUPS), 8)
            for i in range(GROUPS):
                at = pl.ds(start + 8 * i, 8)
                t = [target_ref[c, at, :] for c in range(3)]
                sums = [sums_ref[c, at, :] for c in range(3)]
                for h in range(halves):
                    dx, dy, dz = s[h][0] - t[0], s[h][1] - t[1], s[h][2] - t[2]
                    inv = lax.rsqrt(dx * dx + dy * dy + dz * dz + near_soft)
                    w = s[h][3] * (inv * inv * inv)
                    sums = [sums[0] + dx * w, sums[1] + dy * w, sums[2] + dz * w]
                for c in range(3):
                    sums_ref[c, at, :] = sums[c]
            return carry

        lax.fori_loop(0, (count + 8 * GROUPS - 1) // (8 * GROUPS), chunk, 0)

    def item(k, carry):
        value = control_ref[0, k]
        b, place = value // 32, value % 32
        row = place * 8
        first, count = b * LEAF, control_ref[b, COUNT]
        both = jnp.right_shift(masks_ref[place // BLK], place % BLK) % 2

        @pl.when(both == 1)
        def _():
            run(row, first, count, 2)

        @pl.when(both == 0)
        def _():
            run(row, first, count, 1)

        return carry

    lax.fori_loop(control_ref[0, ITEMS + stage], control_ref[0, ITEMS + stage + 1], item, 0)


def block_of(ref):
    return lambda b: ref[b * 8 : b * 8 + 8, :]


def near_one_kernel(control_ref, own, wide_a, wide_b, sums_ref, target_ref, source_ref, masks_ref):
    spread_targets(own, target_ref)
    sums_ref[...] = jnp.zeros_like(sums_ref)
    bodies = [*map(block_of, (own, wide_a, wide_b))]
    near_part(control_ref, target_ref, sums_ref, source_ref, masks_ref, bodies, 0)


def near_two_kernel(control_ref, wide_a, wide_b, wide_c, mine, before, target_ref, sums_ref, source_ref, masks_ref):
    spread_targets(mine, target_ref)
    bodies = [*map(block_of, (wide_a, wide_b, wide_c))]
    near_part(control_ref, target_ref, sums_ref, source_ref, masks_ref, bodies, 1)


def near_three_kernel(control_ref, z_one, y_all, target_ref, before, out_ref, sums_ref, source_ref, masks_ref):
    y = lax.axis_index("oct") // 4

    def member(flip):
        return lambda b: y_all[y ^ flip, b * 8 : b * 8 + 8, :]

    bodies = [block_of(z_one), member(1), member(2)]
    near_part(control_ref, target_ref, sums_ref, source_ref, masks_ref, bodies, 2)
    lane8 = lax.broadcasted_iota(I32, (LEAF, BLK), 1)
    for c in range(3):
        columns = jnp.zeros((LEAF, BLK), F32)
        for b in range(BLK):
            part = jnp.sum(sums_ref[c, b * LEAF : (b + 1) * LEAF, :], axis=1, keepdims=True)
            columns = jnp.where(lane8 == b, part, columns)
        out_ref[c] = columns.T


def three_parts(a):
    hi = a.astype(jnp.bfloat16)
    rest = a - hi.astype(F32)
    mid = rest.astype(jnp.bfloat16)
    return hi, mid, (rest - mid.astype(F32)).astype(jnp.bfloat16)


def last_items(control_ref, own, body_ref, sums_ref, flipped_ref, stage):
    lane8 = lax.broadcasted_iota(I32, (BLK, 128), 1)
    block8 = lax.broadcasted_iota(I32, (BLK, 128), 0)
    second = body_ref[pl.ds(7, BLK, stride=8), :]
    mask = jnp.sum(jnp.where((lane8 == 0) & (second > 0.0), jnp.left_shift(1, block8), 0))
    for b in range(BLK):
        flipped_ref[b] = body_ref[b * 8 : b * 8 + 8, :].T

    def item(k, carry):
        value = control_ref[0, k]
        b, slot = value // 32, value % 32

        def run(h):
            acc = [jnp.zeros((8, 128), F32)] * 6
            t = [
                [jnp.broadcast_to(own[pl.ds(b * 8 + half * 4 + c, 1), :], (8, 128)) for c in range(3)]
                for half in range(2)
            ]
            for i in range(16):
                columns = flipped_ref[slot, 8 * i : 8 * i + 8, :]
                s = [jnp.broadcast_to(columns[:, h * 4 + c : h * 4 + c + 1], (8, 128)) for c in range(4)]
                for half in range(2):
                    dx, dy, dz = s[0] - t[half][0], s[1] - t[half][1], s[2] - t[half][2]
                    inv = lax.rsqrt(dx * dx + dy * dy + dz * dz + near_soft)
                    w = s[3] * (inv * inv * inv)
                    acc[3 * half] += dx * w
                    acc[3 * half + 1] += dy * w
                    acc[3 * half + 2] += dz * w
            for half in range(2):
                for c in range(3):
                    total = jnp.sum(acc[3 * half + c], axis=0, keepdims=True)
                    sums_ref[c * 2 + half, pl.ds(b, 1), :] += total

        run(0)

        @pl.when(jnp.right_shift(mask, slot) % 2 == 1)
        def _():
            run(1)

        return carry

    lax.fori_loop(control_ref[0, ITEMS + stage], control_ref[0, ITEMS + stage + 1], item, 0)


def last_kernel(control_ref, far_ref, own, z_one, z_two, before, out_ref, sums_ref, table_ref, rows_ref, flipped_ref, *, entries):
    for c in range(3):
        for half in range(2):
            sums_ref[2 * c + half] = before[c, :, half * 128 : half * 128 + 128]
    last_items(control_ref, own, z_two, sums_ref, flipped_ref, 3)
    sums = [jnp.concatenate([sums_ref[2 * c], sums_ref[2 * c + 1]], axis=1) for c in range(3)]
    me = lax.axis_index("oct") % 4
    other = 3 - me
    n = z_one.shape[0] - BODY
    for place, rows in (
        (me, own[BODY:, :]),
        (me ^ 1, z_one[BODY:, :]),
        (other, z_two[BODY : BODY + n, :]),
        (other ^ 1, z_two[BODY + n :, :]),
    ):
        table_ref[pl.ds(pl.multiple_of(place * n, n), n), :] = rows
    members = lax.axis_size("oct")
    far_count = far_ref.shape[1]
    picks = BLK * far_count
    lanes = lax.broadcasted_iota(I32, (picks, 128), 1)
    code = jnp.concatenate([jnp.broadcast_to(far_ref[:, v : v + 1], (BLK, 128)) for v in range(far_count)], axis=0)
    group, member, slot = code // (BLK * members), code // BLK % members, code % BLK
    row = member % 4 * n + member // 4 * 4
    table = jnp.concatenate(three_parts(table_ref[...]), axis=1)
    folded = jnp.zeros((picks, 128), F32)
    lhs, rhs = [], []
    fold_from = lax.broadcasted_iota(I32, (128, 128), 0)
    fold_to = lax.broadcasted_iota(I32, (128, 128), 1)
    for at_row, low, width, base in (
        (row + group // 2, slot * SLOT + group % 2 * 8, 8, 0),
        (row + 3, slot * SLOT + group * 2, 2, 8),
    ):
        hot = (lanes == at_row)[:, : table_ref.shape[0]].astype(F32).astype(jnp.bfloat16)
        rows = jnp.dot(hot, table, preferred_element_type=F32)
        keep = (lanes >= low) & (lanes < low + width)
        fold = (fold_from % width + base == fold_to).astype(F32).astype(jnp.bfloat16)
        for part in range(3):
            chosen = jnp.where(keep, rows[:, part * 128 : (part + 1) * 128], 0.0)
            lhs.append(chosen.astype(jnp.bfloat16))
            rhs.append(fold)
    folded = jnp.dot(jnp.concatenate(lhs, axis=1), jnp.concatenate(rhs, axis=0), preferred_element_type=F32)
    hi, mid, low = (part.astype(F32) for part in three_parts(folded))
    parts = (hi + pltpu.roll(mid, SLOT, 1) + pltpu.roll(low, 2 * SLOT, 1)).astype(jnp.bfloat16)
    k = lax.broadcasted_iota(I32, (128, 10 * 128), 0)
    n = lax.broadcasted_iota(I32, (128, 10 * 128), 1)
    ones = ((k % SLOT == n // 128) & (k < 3 * SLOT)).astype(F32).astype(jnp.bfloat16)
    spread = jnp.dot(parts, ones, preferred_element_type=F32)
    x, y, z, _ = planes(own)
    for v in range(far_count):
        mass, cx, cy, cz, xx, yy, zz, xy, xz, yz = (
            jnp.concatenate([spread[v * BLK : (v + 1) * BLK, k * 128 : k * 128 + 128]] * 2, axis=1) for k in range(10)
        )
        rx, ry, rz = x - cx, y - cy, z - cz
        inv = lax.rsqrt(rx * rx + ry * ry + rz * rz + far_soft)
        inv2 = inv * inv
        inv3 = inv * inv2
        inv5 = inv3 * inv2
        inv7 = inv5 * inv2
        qx = xx * rx + xy * ry + xz * rz
        qy = xy * rx + yy * ry + yz * rz
        qz = xz * rx + yz * ry + zz * rz
        rqr = rx * qx + ry * qy + rz * qz
        radial = -mass * inv3 - 2.5 * rqr * inv7
        sums[0] += rx * radial + qx * inv5
        sums[1] += ry * radial + qy * inv5
        sums[2] += rz * radial + qz * inv5
    lane = lax.broadcasted_iota(I32, (1, LEAF), 1)
    grav = 1.0 / (entries * LEAF)
    for c in range(3):
        rows_ref[c] = sums[c] * grav
        for b in range(BLK):
            out_ref[c : c + 1, b * LEAF : (b + 1) * LEAF] = jnp.where(lane < control_ref[b, COUNT], rows_ref[c, b : b + 1, :], 0.0)


def sources(sets):
    return [pltpu.VMEM((sets * BODY, 128), F32), pltpu.SMEM((4,), I32)]


def params(mib):
    return pltpu.CompilerParams(vmem_limit_bytes=mib << 20)


def cost(flops):
    return pl.CostEstimate(flops=flops, bytes_accessed=1 << 18, transcendentals=0)


def mine_kernel(own, y_all, out_ref):
    out_ref[:BODY, :] = own[:BODY, :]
    for y in range(4):
        out_ref[BODY + 4 * y : BODY + 4 * y + 4, :] = y_all[y, BODY : BODY + 4, :]


def relay_kernel(mine, z_one, out_ref):
    n = z_one.shape[0] - BODY
    out_ref[:BODY, :] = z_one[:BODY, :]
    out_ref[BODY : BODY + n, :] = mine[BODY:, :]
    out_ref[BODY + n :, :] = z_one[BODY:, :]


def small_call(kernel, rows, *operands):
    return pl.pallas_call(
        kernel,
        out_shape=jax.ShapeDtypeStruct((rows, 128), F32),
        in_specs=[VMEM] * len(operands),
        out_specs=VMEM,
        compiler_params=params(2),
    )(*operands)


def exchange(payload, axis, flip):
    return lax.ppermute(payload, axis, [(i, flip(i)) for i in range(lax.axis_size(axis))])


def step(positions, masses, counts, near_list, far_list):
    wide_bits = lax.axis_size("wide").bit_length() - 1
    shape = (BODY + 8, 128)
    entries = near_list.shape[1]
    own, control = pl.pallas_call(
        pack_kernel,
        out_shape=[jax.ShapeDtypeStruct(shape, F32), jax.ShapeDtypeStruct((BLK, 128), I32)],
        in_specs=[HBM] * 4,
        out_specs=[VMEM, VMEM],
        scratch_shapes=[
            pltpu.SMEM(counts.shape, I32),
            pltpu.VMEM(positions.shape, F32),
            pltpu.VMEM((16, 128), F32),
            pltpu.VMEM(near_list.shape, I32),
            pltpu.SemaphoreType.DMA((4,)),
        ],
        compiler_params=params(4),
        name="pack",
    )(*(pltpu.with_memory_space_constraint(a, pltpu.HBM) for a in (counts, positions, masses.reshape(16, 128), near_list)))
    wide = []
    for bit in range(wide_bits):
        wide.append(exchange(own, "wide", lambda i, bit=bit: i ^ (1 << bit)))
    message = pl.pallas_call(
        join_kernel,
        out_shape=jax.ShapeDtypeStruct((4, *shape), F32),
        in_specs=[VMEM] * (1 + wide_bits),
        out_specs=VMEM,
        compiler_params=params(4),
        name="join",
    )(own, *wide)
    y_groups = [[z + 4 * y for y in range(4)] for z in range(4)]
    y_all = lax.all_to_all(message, "oct", 0, 0, axis_index_groups=y_groups)
    state = jax.ShapeDtypeStruct((3, BLK * LEAF, 128), F32)
    sums = pl.pallas_call(
        near_one_kernel,
        out_shape=state,
        in_specs=[SMEM] + [VMEM] * 3,
        out_specs=VMEM,
        scratch_shapes=[pltpu.VMEM(state.shape, F32), *sources(3)],
        compiler_params=params(8),
        cost_estimate=cost(20 << 20),
        name="near_one",
    )(control, own, wide[0], wide[1])
    mine = small_call(mine_kernel, BODY + 16, own, y_all)
    z_one = exchange(mine, "oct", lambda i: i ^ 1)
    targets, sums = pl.pallas_call(
        near_two_kernel,
        out_shape=[state, state],
        in_specs=[SMEM] + [VMEM] * 5,
        out_specs=[VMEM, VMEM],
        scratch_shapes=sources(3),
        input_output_aliases={5: 1},
        compiler_params=params(8),
        cost_estimate=cost(20 << 20),
        name="near_two",
    )(control, *wide[2:], mine, sums)
    relay = small_call(relay_kernel, BODY + 32, mine, z_one)
    z_two = exchange(relay, "oct", lambda i: (i & ~3) | RELAY[i & 3])
    sums = pl.pallas_call(
        near_three_kernel,
        out_shape=[jax.ShapeDtypeStruct((3, BLK, LEAF), F32), state],
        in_specs=[SMEM] + [VMEM] * 4,
        out_specs=[VMEM, VMEM],
        scratch_shapes=sources(3),
        input_output_aliases={4: 1},
        compiler_params=params(8),
        cost_estimate=cost(20 << 20),
        name="near_three",
    )(control, relay, y_all, targets, sums)[0]
    return pl.pallas_call(
        functools.partial(last_kernel, entries=entries),
        out_shape=jax.ShapeDtypeStruct(positions.shape, F32),
        in_specs=[SMEM] + [VMEM] * 5,
        out_specs=VMEM,
        scratch_shapes=[
            pltpu.VMEM((6, BLK, 128), F32),
            pltpu.VMEM((64, 128), F32),
            pltpu.VMEM((3, BLK, LEAF), F32),
            pltpu.VMEM((BLK, 128, 8), F32),
        ],
        compiler_params=params(8),
        cost_estimate=cost(20 << 20),
        name="last",
    )(control, far_list, mine, z_one, z_two, sums)


def solution(mesh):
    return jax.shard_map(
        step,
        mesh=mesh,
        in_specs=(
            P(None, ("wide", "oct")),
            P(("wide", "oct")),
            P(("wide", "oct")),
            P(("wide", "oct"), None),
            P(("wide", "oct"), None),
        ),
        out_specs=P(None, ("wide", "oct")),
        check_vma=False,
    )
```

```python
import functools

import jax
import jax.numpy as jnp
from jax import lax
from jax.experimental import pallas as pl
from jax.experimental.pallas import tpu as pltpu
from jax.sharding import PartitionSpec as P


near_soft = 0.01
far_soft = 0.25
BLK = 8
LEAF = 256
BODY = BLK * 8
STEP = 32
FEWEST = 3
SLOT = 16
F32 = jnp.float32
I32 = jnp.int32
VMEM = pl.BlockSpec(memory_space=pltpu.VMEM)
SMEM = pl.BlockSpec(memory_space=pltpu.SMEM)
HBM = pl.BlockSpec(memory_space=pltpu.HBM)
RELAY = (3, 2, 1, 0)
COUNT = 127
ITEMS = 64
STAGES = ((0, 5, 6), (7, 8, 9), (1, 3, 4), (2,))


def planes(ref):
    half = [[ref[pl.ds(h * 4 + c, BLK, stride=8), :] for h in range(2)] for c in range(4)]
    return [jnp.concatenate(pair, axis=1) for pair in half]


def pack_kernel(counts_hbm, pos_hbm, mass_hbm, near_hbm, out_ref, control_ref, counts_ref, pos_ref, mass_ref, near_ref, sems):
    moves = ((pos_hbm, pos_ref), (mass_hbm, mass_ref), (counts_hbm, counts_ref), (near_hbm, near_ref))
    copies = [pltpu.make_async_copy(src, dst, sems.at[i]) for i, (src, dst) in enumerate(moves)]
    for copy in copies:
        copy.start()
    for copy in copies:
        copy.wait()
    lane = lax.broadcasted_iota(I32, (1, 128), 1)
    for b in range(BLK):
        for half in range(2):
            row = b * 8 + half * 4
            at = b * LEAF + half * 128
            for c in range(3):
                out_ref[row + c : row + c + 1, :] = pos_ref[c : c + 1, at : at + 128]
            live = lane + half * 128 < counts_ref[b]
            out_ref[row + 3 : row + 4, :] = jnp.where(live, mass_ref[2 * b + half : 2 * b + half + 1, :], 0.0)
    x, y, z, m = planes(out_ref)

    def total(a):
        return jnp.sum(a, axis=1, keepdims=True)

    mass = total(m)
    cx, cy, cz = total(x * m) / mass, total(y * m) / mass, total(z * m) / mass
    dx, dy, dz = x - cx, y - cy, z - cz
    mx, my, mz = m * dx, m * dy, m * dz
    xx, yy, zz = total(mx * dx), total(my * dy), total(mz * dz)
    trace = xx + yy + zz
    first = [mass, cx, cy, cz, 3.0 * xx - trace, 3.0 * yy - trace, 3.0 * zz - trace, 3.0 * total(mx * dy)]
    last = [3.0 * total(mx * dz), 3.0 * total(my * dz)]
    lanes = lax.broadcasted_iota(I32, (BLK, 128), 1)
    blocks = lax.broadcasted_iota(I32, (BLK, 128), 0)

    def cell_row(columns):
        tile = jnp.zeros((BLK, 128), F32)
        for k, column in enumerate(columns):
            tile = jnp.where(lanes % SLOT == k, column, tile)
        return jnp.sum(jnp.where(lanes // SLOT == blocks, tile, 0.0), axis=0, keepdims=True)

    rows = jnp.where(blocks == 0, cell_row(first), 0.0)
    out_ref[BODY:, :] = jnp.where(blocks == 1, cell_row(last), rows)
    code = near_ref[...]
    entries = code.shape[1]
    stage = jnp.zeros_like(code)
    value = lax.broadcasted_iota(I32, code.shape, 0) * 32 + code % BLK
    for number, names in enumerate(STAGES):
        for place, name in enumerate(names):
            stage = jnp.where(code // BLK == name, number, stage)
            value = value + jnp.where(code // BLK == name, place * BLK, 0)

    def column(a):
        return jnp.concatenate([jnp.broadcast_to(a[:, v : v + 1], (BLK, 128)) for v in range(entries)], axis=0).astype(F32)

    stages = column(stage)
    items = BLK * entries
    down = lax.broadcasted_iota(I32, (items, 128), 0).astype(F32)
    across = lax.broadcasted_iota(I32, (items, 128), 1).astype(F32)
    key = stages * items + down
    rank = jnp.sum((key.T[:items, :] < key[:, :items]).astype(F32), axis=1, keepdims=True)
    sorted_items = jnp.where(rank == across, column(value), 0.0)
    starts = (stages < across - ITEMS).astype(F32)
    row = jnp.sum(jnp.where(across < ITEMS, sorted_items, starts), axis=0, keepdims=True).astype(I32)
    control = jnp.where(blocks == 0, row, 0)
    for b in range(BLK):
        control = jnp.where((blocks == b) & (lanes == COUNT), counts_ref[b], control)
    control_ref[...] = control


def other_core():
    return 1 - lax.axis_index("wide") % 2


def join_kernel(*refs):
    own, pair, *others, out_ref = refs
    sets = [own, pair.at[other_core()], *others]
    first = [ref[BODY : BODY + 1, :] for ref in sets]
    last = sum(pltpu.roll(jnp.broadcast_to(ref[BODY + 1 : BODY + 2, :], (8, 128)), 2 * g, 1) if g else jnp.broadcast_to(ref[BODY + 1 : BODY + 2, :], (8, 128)) for g, ref in enumerate(sets))
    at = lax.broadcasted_iota(I32, (8, 128), 0)
    tile = jnp.where(at == 3, last, 0.0)
    for g in range(0, len(sets), 2):
        pair = jnp.broadcast_to(first[g], (8, 128))
        if g + 1 < len(sets):
            pair = pair + pltpu.roll(jnp.broadcast_to(first[g + 1], (8, 128)), 8, 1)
        tile = jnp.where(at == g // 2, pair, tile)
    for k in range(out_ref.shape[0]):
        out_ref[k, :BODY, :] = sets[0][:BODY, :]
        out_ref[k, BODY:, :] = tile


def spread_targets(own, target_ref):
    k = lax.broadcasted_iota(I32, (3 * BLK, BLK * 128), 0)
    n = lax.broadcasted_iota(I32, (3 * BLK, BLK * 128), 1)
    ones = (k % BLK == n // 128).astype(F32).astype(jnp.bfloat16)
    for c, plane in enumerate(planes(own)[:3]):
        parts = jnp.concatenate([part.astype(F32) for part in three_parts(plane)], axis=0).astype(jnp.bfloat16)
        spread = lax.dot_general(parts, ones, (((0,), (0,)), ((), ())), preferred_element_type=F32)
        for b in range(BLK):
            target_ref[c, b * LEAF : (b + 1) * LEAF, :] = spread[:, b * 128 : (b + 1) * 128]


def near_part(control_ref, target_ref, sums_ref, source_ref, masks_ref, bodies, stage):
    lane8 = lax.broadcasted_iota(I32, (BLK, 128), 1)
    block8 = lax.broadcasted_iota(I32, (BLK, 128), 0)
    for s, body in enumerate(bodies):
        for b in range(BLK):
            source_ref[s * BODY + b * 8 : s * BODY + b * 8 + 8, :] = body(b)
    for s in range(len(bodies)):
        second = source_ref[pl.ds(s * BODY + 7, BLK, stride=8), :]
        masks_ref[s] = jnp.sum(jnp.where((lane8 == 0) & (second > 0.0), jnp.left_shift(1, block8), 0))

    last = jnp.int32(ITEMS - 1)

    def decode(k):
        value = control_ref[0, jnp.minimum(k, last)]
        b, place = value // 32, value % 32
        steps = (control_ref[b, COUNT] + STEP - 1) // STEP
        both = jnp.right_shift(masks_ref[place // BLK], place % BLK) % 2
        return place * 8, b * LEAF, jnp.maximum(steps - FEWEST, 0), both

    def run(steps, halves, k, row, first):
        s = [
            [jnp.broadcast_to(source_ref[pl.ds(row + 4 * h + c, 1), :], (8, 128)) for c in range(4)]
            for h in range(halves)
        ]
        first = pl.multiple_of(first, LEAF)
        for i in range(steps * STEP // 8):
            at = pl.ds(first + 8 * i, 8)
            t = [target_ref[c, at, :] for c in range(3)]
            sums = [sums_ref[c, at, :] for c in range(3)]
            for h in range(halves):
                dx, dy, dz = s[h][0] - t[0], s[h][1] - t[1], s[h][2] - t[2]
                inv = lax.rsqrt(dx * dx + dy * dy + dz * dz + near_soft)
                w = s[h][3] * (inv * inv * inv)
                sums = [sums[0] + dx * w, sums[1] + dy * w, sums[2] + dz * w]
            for c in range(3):
                sums_ref[c, at, :] = sums[c]
        return decode(k + 1)

    def choose(low, high, halves, k, row, first, extra):
        if low == high:
            return run(low + FEWEST, halves, k, row, first)
        mid = (low + high) // 2
        return lax.cond(
            extra <= mid,
            lambda: choose(low, mid, halves, k, row, first, extra),
            lambda: choose(mid + 1, high, halves, k, row, first, extra),
        )

    def item(k, now):
        row, first, extra, both = now
        most = LEAF // STEP - FEWEST
        return lax.cond(
            both == 1,
            lambda: choose(0, most, 2, k, row, first, extra),
            lambda: choose(0, most, 1, k, row, first, extra),
        )

    begin = control_ref[0, ITEMS + stage]
    lax.fori_loop(begin, control_ref[0, ITEMS + stage + 1], item, decode(begin))


def block_of(ref):
    return lambda b: ref[b * 8 : b * 8 + 8, :]


def near_one_kernel(control_ref, own, pair, wide_a, sums_ref, target_ref, source_ref, masks_ref):
    spread_targets(own, target_ref)
    sums_ref[...] = jnp.zeros_like(sums_ref)
    bodies = [block_of(own), block_of(pair.at[other_core()]), block_of(wide_a)]
    near_part(control_ref, target_ref, sums_ref, source_ref, masks_ref, bodies, 0)


def near_two_kernel(control_ref, wide_a, wide_b, wide_c, mine, before, target_ref, sums_ref, source_ref, masks_ref):
    spread_targets(mine, target_ref)
    bodies = [*map(block_of, (wide_a, wide_b, wide_c))]
    near_part(control_ref, target_ref, sums_ref, source_ref, masks_ref, bodies, 1)


def near_three_kernel(control_ref, z_one, y_all, target_ref, before, out_ref, sums_ref, source_ref, masks_ref):
    y = lax.axis_index("oct") // 4

    def member(flip):
        return lambda b: y_all[y ^ flip, b * 8 : b * 8 + 8, :]

    bodies = [block_of(z_one), member(1), member(2)]
    near_part(control_ref, target_ref, sums_ref, source_ref, masks_ref, bodies, 2)
    lane8 = lax.broadcasted_iota(I32, (LEAF, BLK), 1)
    for c in range(3):
        columns = jnp.zeros((LEAF, BLK), F32)
        for b in range(BLK):
            part = jnp.sum(sums_ref[c, b * LEAF : (b + 1) * LEAF, :], axis=1, keepdims=True)
            columns = jnp.where(lane8 == b, part, columns)
        out_ref[c] = columns.T


def three_parts(a):
    hi = a.astype(jnp.bfloat16)
    rest = a - hi.astype(F32)
    mid = rest.astype(jnp.bfloat16)
    return hi, mid, (rest - mid.astype(F32)).astype(jnp.bfloat16)


def last_items(control_ref, own, body_ref, sums_ref, flipped_ref, spread_ref, stage):
    lane8 = lax.broadcasted_iota(I32, (BLK, 128), 1)
    block8 = lax.broadcasted_iota(I32, (BLK, 128), 0)
    second = body_ref[pl.ds(7, BLK, stride=8), :]
    mask = jnp.sum(jnp.where((lane8 == 0) & (second > 0.0), jnp.left_shift(1, block8), 0))
    for b in range(BLK):
        flipped_ref[b] = body_ref[b * 8 : b * 8 + 8, :].T

    def item(k, carry):
        value = control_ref[0, k]
        b, slot = value // 32, value % 32

        def run(h):
            acc = [jnp.zeros((8, 128), F32)] * 6
            t = [
                [jnp.broadcast_to(own[pl.ds(b * 8 + half * 4 + c, 1), :], (8, 128)) for c in range(3)]
                for half in range(2)
            ]
            for c in range(4):
                for i in range(16):
                    column = flipped_ref[slot, 8 * i : 8 * i + 8, h * 4 + c : h * 4 + c + 1]
                    spread_ref[c, 8 * i : 8 * i + 8, :] = jnp.broadcast_to(column, (8, 128))
            for i in range(16):
                s = [spread_ref[c, 8 * i : 8 * i + 8, :] for c in range(4)]
                for half in range(2):
                    dx, dy, dz = s[0] - t[half][0], s[1] - t[half][1], s[2] - t[half][2]
                    inv = lax.rsqrt(dx * dx + dy * dy + dz * dz + near_soft)
                    w = s[3] * (inv * inv * inv)
                    acc[3 * half] += dx * w
                    acc[3 * half + 1] += dy * w
                    acc[3 * half + 2] += dz * w
            for half in range(2):
                for c in range(3):
                    total = jnp.sum(acc[3 * half + c], axis=0, keepdims=True)
                    sums_ref[c * 2 + half, pl.ds(b, 1), :] += total

        run(0)

        @pl.when(jnp.right_shift(mask, slot) % 2 == 1)
        def _():
            run(1)

        return carry

    lax.fori_loop(control_ref[0, ITEMS + stage], control_ref[0, ITEMS + stage + 1], item, 0)


def last_kernel(control_ref, far_ref, own, z_one, z_two, before, out_ref, sums_ref, table_ref, rows_ref, flipped_ref, spread_ref, *, entries):
    for c in range(3):
        for half in range(2):
            sums_ref[2 * c + half] = before[c, :, half * 128 : half * 128 + 128]
    last_items(control_ref, own, z_two, sums_ref, flipped_ref, spread_ref, 3)
    sums = [jnp.concatenate([sums_ref[2 * c], sums_ref[2 * c + 1]], axis=1) for c in range(3)]
    me = lax.axis_index("oct") % 4
    other = 3 - me
    n = z_one.shape[0] - BODY
    for place, rows in (
        (me, own[BODY:, :]),
        (me ^ 1, z_one[BODY:, :]),
        (other, z_two[BODY : BODY + n, :]),
        (other ^ 1, z_two[BODY + n :, :]),
    ):
        table_ref[pl.ds(pl.multiple_of(place * n, n), n), :] = rows
    members = lax.axis_size("oct")
    far_count = far_ref.shape[1]
    picks = BLK * far_count
    lanes = lax.broadcasted_iota(I32, (picks, 128), 1)
    code = jnp.concatenate([jnp.broadcast_to(far_ref[:, v : v + 1], (BLK, 128)) for v in range(far_count)], axis=0)
    group, member, slot = code // (BLK * members), code // BLK % members, code % BLK
    row = member % 4 * n + member // 4 * 4
    table = jnp.concatenate(three_parts(table_ref[...]), axis=1)
    folded = jnp.zeros((picks, 128), F32)
    lhs, rhs = [], []
    fold_from = lax.broadcasted_iota(I32, (128, 128), 0)
    fold_to = lax.broadcasted_iota(I32, (128, 128), 1)
    for at_row, low, width, base in (
        (row + group // 2, slot * SLOT + group % 2 * 8, 8, 0),
        (row + 3, slot * SLOT + group * 2, 2, 8),
    ):
        hot = (lanes == at_row)[:, : table_ref.shape[0]].astype(F32).astype(jnp.bfloat16)
        rows = jnp.dot(hot, table, preferred_element_type=F32)
        keep = (lanes >= low) & (lanes < low + width)
        fold = (fold_from % width + base == fold_to).astype(F32).astype(jnp.bfloat16)
        for part in range(3):
            chosen = jnp.where(keep, rows[:, part * 128 : (part + 1) * 128], 0.0)
            lhs.append(chosen.astype(jnp.bfloat16))
            rhs.append(fold)
    folded = jnp.dot(jnp.concatenate(lhs, axis=1), jnp.concatenate(rhs, axis=0), preferred_element_type=F32)
    hi, mid, low = (part.astype(F32) for part in three_parts(folded))
    parts = (hi + pltpu.roll(mid, SLOT, 1) + pltpu.roll(low, 2 * SLOT, 1)).astype(jnp.bfloat16)
    k = lax.broadcasted_iota(I32, (128, 10 * 128), 0)
    n = lax.broadcasted_iota(I32, (128, 10 * 128), 1)
    ones = ((k % SLOT == n // 128) & (k < 3 * SLOT)).astype(F32).astype(jnp.bfloat16)
    spread = jnp.dot(parts, ones, preferred_element_type=F32)
    x, y, z, _ = planes(own)
    for v in range(far_count):
        mass, cx, cy, cz, xx, yy, zz, xy, xz, yz = (
            jnp.concatenate([spread[v * BLK : (v + 1) * BLK, k * 128 : k * 128 + 128]] * 2, axis=1) for k in range(10)
        )
        rx, ry, rz = x - cx, y - cy, z - cz
        inv = lax.rsqrt(rx * rx + ry * ry + rz * rz + far_soft)
        inv2 = inv * inv
        inv3 = inv * inv2
        inv5 = inv3 * inv2
        inv7 = inv5 * inv2
        qx = xx * rx + xy * ry + xz * rz
        qy = xy * rx + yy * ry + yz * rz
        qz = xz * rx + yz * ry + zz * rz
        rqr = rx * qx + ry * qy + rz * qz
        radial = -mass * inv3 - 2.5 * rqr * inv7
        sums[0] += rx * radial + qx * inv5
        sums[1] += ry * radial + qy * inv5
        sums[2] += rz * radial + qz * inv5
    lane = lax.broadcasted_iota(I32, (1, LEAF), 1)
    grav = 1.0 / (entries * LEAF)
    for c in range(3):
        rows_ref[c] = sums[c] * grav
        for b in range(BLK):
            out_ref[c : c + 1, b * LEAF : (b + 1) * LEAF] = jnp.where(lane < control_ref[b, COUNT], rows_ref[c, b : b + 1, :], 0.0)


def sources(sets):
    return [pltpu.VMEM((sets * BODY, 128), F32), pltpu.SMEM((4,), I32)]


def params(mib):
    return pltpu.CompilerParams(vmem_limit_bytes=mib << 20)


def cost(flops):
    return pl.CostEstimate(flops=flops, bytes_accessed=1 << 18, transcendentals=0)


def mine_kernel(own, y_all, out_ref):
    out_ref[:BODY, :] = own[:BODY, :]
    for y in range(4):
        out_ref[BODY + 4 * y : BODY + 4 * y + 4, :] = y_all[y, BODY : BODY + 4, :]


def relay_kernel(mine, z_one, out_ref):
    n = z_one.shape[0] - BODY
    out_ref[:BODY, :] = z_one[:BODY, :]
    out_ref[BODY : BODY + n, :] = mine[BODY:, :]
    out_ref[BODY + n :, :] = z_one[BODY:, :]


def small_call(kernel, rows, *operands):
    return pl.pallas_call(
        kernel,
        out_shape=jax.ShapeDtypeStruct((rows, 128), F32),
        in_specs=[VMEM] * len(operands),
        out_specs=VMEM,
        compiler_params=params(2),
    )(*operands)


def exchange(payload, axis, flip):
    return lax.ppermute(payload, axis, [(i, flip(i)) for i in range(lax.axis_size(axis))])


def step(positions, masses, counts, near_list, far_list):
    wide_bits = lax.axis_size("wide").bit_length() - 1
    shape = (BODY + 8, 128)
    entries = near_list.shape[1]
    own, control = pl.pallas_call(
        pack_kernel,
        out_shape=[jax.ShapeDtypeStruct(shape, F32), jax.ShapeDtypeStruct((BLK, 128), I32)],
        in_specs=[HBM] * 4,
        out_specs=[VMEM, VMEM],
        scratch_shapes=[
            pltpu.SMEM(counts.shape, I32),
            pltpu.VMEM(positions.shape, F32),
            pltpu.VMEM((16, 128), F32),
            pltpu.VMEM(near_list.shape, I32),
            pltpu.SemaphoreType.DMA((4,)),
        ],
        compiler_params=params(4),
        name="pack",
    )(*(pltpu.with_memory_space_constraint(a, pltpu.HBM) for a in (counts, positions, masses.reshape(16, 128), near_list)))
    wide = []
    cores = [[i, i + 1] for i in range(0, lax.axis_size("wide"), 2)]
    pair = lax.all_gather(own, "wide", axis_index_groups=cores)
    for bit in range(1, wide_bits):
        wide.append(exchange(own, "wide", lambda i, bit=bit: i ^ (1 << bit)))
    message = pl.pallas_call(
        join_kernel,
        out_shape=jax.ShapeDtypeStruct((4, *shape), F32),
        in_specs=[VMEM] * (1 + wide_bits),
        out_specs=VMEM,
        compiler_params=params(4),
        name="join",
    )(own, pair, *wide)
    y_groups = [[z + 4 * y for y in range(4)] for z in range(4)]
    y_all = lax.all_to_all(message, "oct", 0, 0, axis_index_groups=y_groups)
    state = jax.ShapeDtypeStruct((3, BLK * LEAF, 128), F32)
    sums = pl.pallas_call(
        near_one_kernel,
        out_shape=state,
        in_specs=[SMEM] + [VMEM] * 3,
        out_specs=VMEM,
        scratch_shapes=[pltpu.VMEM(state.shape, F32), *sources(3)],
        compiler_params=params(8),
        cost_estimate=cost(20 << 20),
        name="near_one",
    )(control, own, pair, wide[0])
    mine = small_call(mine_kernel, BODY + 16, own, y_all)
    z_one = exchange(mine, "oct", lambda i: i ^ 1)
    targets, sums = pl.pallas_call(
        near_two_kernel,
        out_shape=[state, state],
        in_specs=[SMEM] + [VMEM] * 5,
        out_specs=[VMEM, VMEM],
        scratch_shapes=sources(3),
        input_output_aliases={5: 1},
        compiler_params=params(8),
        cost_estimate=cost(20 << 20),
        name="near_two",
    )(control, *wide[1:], mine, sums)
    relay = small_call(relay_kernel, BODY + 32, mine, z_one)
    z_two = exchange(relay, "oct", lambda i: (i & ~3) | RELAY[i & 3])
    sums = pl.pallas_call(
        near_three_kernel,
        out_shape=[jax.ShapeDtypeStruct((3, BLK, LEAF), F32), state],
        in_specs=[SMEM] + [VMEM] * 4,
        out_specs=[VMEM, VMEM],
        scratch_shapes=sources(3),
        input_output_aliases={4: 1},
        compiler_params=params(8),
        cost_estimate=cost(20 << 20),
        name="near_three",
    )(control, relay, y_all, targets, sums)[0]
    return pl.pallas_call(
        functools.partial(last_kernel, entries=entries),
        out_shape=jax.ShapeDtypeStruct(positions.shape, F32),
        in_specs=[SMEM] + [VMEM] * 5,
        out_specs=VMEM,
        scratch_shapes=[
            pltpu.VMEM((6, BLK, 128), F32),
            pltpu.VMEM((64, 128), F32),
            pltpu.VMEM((3, BLK, LEAF), F32),
            pltpu.VMEM((BLK, 128, 8), F32),
            pltpu.VMEM((4, 128, 128), F32),
        ],
        compiler_params=params(8),
        cost_estimate=cost(20 << 20),
        name="last",
    )(control, far_list, mine, z_one, z_two, sums)


def solution(mesh):
    return jax.shard_map(
        step,
        mesh=mesh,
        in_specs=(
            P(None, ("wide", "oct")),
            P(("wide", "oct")),
            P(("wide", "oct")),
            P(("wide", "oct"), None),
            P(("wide", "oct"), None),
        ),
        out_specs=P(None, ("wide", "oct")),
        check_vma=False,
    )
```

```python
import functools

import jax
import jax.numpy as jnp
from jax import lax
from jax.experimental import pallas as pl
from jax.experimental.pallas import tpu as pltpu
from jax.sharding import PartitionSpec as P


near_soft = 0.01
far_soft = 0.25
BLK = 8
LEAF = 256
BODY = BLK * 8
STEP = 32
FEWEST = 3
SLOT = 16
F32 = jnp.float32
I32 = jnp.int32
VMEM = pl.BlockSpec(memory_space=pltpu.VMEM)
SMEM = pl.BlockSpec(memory_space=pltpu.SMEM)
HBM = pl.BlockSpec(memory_space=pltpu.HBM)
RELAY = (3, 2, 1, 0)
COUNT = 127
ITEMS = 64
STAGES = ((0, 5, 6, 7), (8, 9), (1, 3, 4), (2,))


def planes(ref):
    half = [[ref[pl.ds(h * 4 + c, BLK, stride=8), :] for h in range(2)] for c in range(4)]
    return [jnp.concatenate(pair, axis=1) for pair in half]


def pack_kernel(counts_hbm, pos_hbm, mass_hbm, near_hbm, out_ref, control_ref, counts_ref, pos_ref, mass_ref, near_ref, sems):
    moves = ((pos_hbm, pos_ref), (mass_hbm, mass_ref), (counts_hbm, counts_ref), (near_hbm, near_ref))
    copies = [pltpu.make_async_copy(src, dst, sems.at[i]) for i, (src, dst) in enumerate(moves)]
    for copy in copies:
        copy.start()
    for copy in copies:
        copy.wait()
    lane = lax.broadcasted_iota(I32, (1, 128), 1)
    for b in range(BLK):
        for half in range(2):
            row = b * 8 + half * 4
            at = b * LEAF + half * 128
            for c in range(3):
                out_ref[row + c : row + c + 1, :] = pos_ref[c : c + 1, at : at + 128]
            live = lane + half * 128 < counts_ref[b]
            out_ref[row + 3 : row + 4, :] = jnp.where(live, mass_ref[2 * b + half : 2 * b + half + 1, :], 0.0)
    x, y, z, m = planes(out_ref)

    def total(a):
        return jnp.sum(a, axis=1, keepdims=True)

    mass = total(m)
    cx, cy, cz = total(x * m) / mass, total(y * m) / mass, total(z * m) / mass
    dx, dy, dz = x - cx, y - cy, z - cz
    mx, my, mz = m * dx, m * dy, m * dz
    xx, yy, zz = total(mx * dx), total(my * dy), total(mz * dz)
    trace = xx + yy + zz
    first = [mass, cx, cy, cz, 3.0 * xx - trace, 3.0 * yy - trace, 3.0 * zz - trace, 3.0 * total(mx * dy)]
    last = [3.0 * total(mx * dz), 3.0 * total(my * dz)]
    lanes = lax.broadcasted_iota(I32, (BLK, 128), 1)
    blocks = lax.broadcasted_iota(I32, (BLK, 128), 0)

    def cell_row(columns):
        tile = jnp.zeros((BLK, 128), F32)
        for k, column in enumerate(columns):
            tile = jnp.where(lanes % SLOT == k, column, tile)
        return jnp.sum(jnp.where(lanes // SLOT == blocks, tile, 0.0), axis=0, keepdims=True)

    rows = jnp.where(blocks == 0, cell_row(first), 0.0)
    out_ref[BODY:, :] = jnp.where(blocks == 1, cell_row(last), rows)
    code = near_ref[...]
    entries = code.shape[1]
    stage = jnp.zeros_like(code)
    value = lax.broadcasted_iota(I32, code.shape, 0) * 32 + code % BLK
    for number, names in enumerate(STAGES):
        for place, name in enumerate(names):
            stage = jnp.where(code // BLK == name, number, stage)
            value = value + jnp.where(code // BLK == name, place * BLK, 0)

    def column(a):
        return jnp.concatenate([jnp.broadcast_to(a[:, v : v + 1], (BLK, 128)) for v in range(entries)], axis=0).astype(F32)

    stages = column(stage)
    items = BLK * entries
    down = lax.broadcasted_iota(I32, (items, 128), 0).astype(F32)
    across = lax.broadcasted_iota(I32, (items, 128), 1).astype(F32)
    key = stages * items + down
    rank = jnp.sum((key.T[:items, :] < key[:, :items]).astype(F32), axis=1, keepdims=True)
    sorted_items = jnp.where(rank == across, column(value), 0.0)
    starts = (stages < across - ITEMS).astype(F32)
    row = jnp.sum(jnp.where(across < ITEMS, sorted_items, starts), axis=0, keepdims=True).astype(I32)
    control = jnp.where(blocks == 0, row, 0)
    for b in range(BLK):
        control = jnp.where((blocks == b) & (lanes == COUNT), counts_ref[b], control)
    control_ref[...] = control


def other_core():
    return 1 - lax.axis_index("wide") % 2


def join_kernel(*refs):
    own, pair, *others, out_ref = refs
    sets = [own, pair.at[other_core()], *others]
    first = [ref[BODY : BODY + 1, :] for ref in sets]
    last = sum(pltpu.roll(jnp.broadcast_to(ref[BODY + 1 : BODY + 2, :], (8, 128)), 2 * g, 1) if g else jnp.broadcast_to(ref[BODY + 1 : BODY + 2, :], (8, 128)) for g, ref in enumerate(sets))
    at = lax.broadcasted_iota(I32, (8, 128), 0)
    tile = jnp.where(at == 3, last, 0.0)
    for g in range(0, len(sets), 2):
        pair = jnp.broadcast_to(first[g], (8, 128))
        if g + 1 < len(sets):
            pair = pair + pltpu.roll(jnp.broadcast_to(first[g + 1], (8, 128)), 8, 1)
        tile = jnp.where(at == g // 2, pair, tile)
    for k in range(out_ref.shape[0]):
        out_ref[k, :BODY, :] = sets[0][:BODY, :]
        out_ref[k, BODY:, :] = tile


def spread_targets(own, target_ref):
    k = lax.broadcasted_iota(I32, (3 * BLK, BLK * 128), 0)
    n = lax.broadcasted_iota(I32, (3 * BLK, BLK * 128), 1)
    ones = (k % BLK == n // 128).astype(F32).astype(jnp.bfloat16)
    for c, plane in enumerate(planes(own)[:3]):
        parts = jnp.concatenate([part.astype(F32) for part in three_parts(plane)], axis=0).astype(jnp.bfloat16)
        spread = lax.dot_general(parts, ones, (((0,), (0,)), ((), ())), preferred_element_type=F32)
        for b in range(BLK):
            target_ref[c, b * LEAF : (b + 1) * LEAF, :] = spread[:, b * 128 : (b + 1) * 128]


def near_part(control_ref, target_ref, sums_ref, source_ref, masks_ref, bodies, stage):
    lane8 = lax.broadcasted_iota(I32, (BLK, 128), 1)
    block8 = lax.broadcasted_iota(I32, (BLK, 128), 0)
    for s, body in enumerate(bodies):
        for b in range(BLK):
            source_ref[s * BODY + b * 8 : s * BODY + b * 8 + 8, :] = body(b)
    for s in range(len(bodies)):
        second = source_ref[pl.ds(s * BODY + 7, BLK, stride=8), :]
        masks_ref[s] = jnp.sum(jnp.where((lane8 == 0) & (second > 0.0), jnp.left_shift(1, block8), 0))

    last = jnp.int32(ITEMS - 1)

    def decode(k):
        value = control_ref[0, jnp.minimum(k, last)]
        b, place = value // 32, value % 32
        steps = (control_ref[b, COUNT] + STEP - 1) // STEP
        both = jnp.right_shift(masks_ref[place // BLK], place % BLK) % 2
        return place * 8, b * LEAF, jnp.maximum(steps - FEWEST, 0), both

    def run(steps, halves, k, row, first):
        s = [
            [jnp.broadcast_to(source_ref[pl.ds(row + 4 * h + c, 1), :], (8, 128)) for c in range(4)]
            for h in range(halves)
        ]
        first = pl.multiple_of(first, LEAF)
        for i in range(steps * STEP // 8):
            at = pl.ds(first + 8 * i, 8)
            t = [target_ref[c, at, :] for c in range(3)]
            sums = [sums_ref[c, at, :] for c in range(3)]
            for h in range(halves):
                dx, dy, dz = s[h][0] - t[0], s[h][1] - t[1], s[h][2] - t[2]
                inv = lax.rsqrt(dx * dx + dy * dy + dz * dz + near_soft)
                w = s[h][3] * (inv * inv * inv)
                sums = [sums[0] + dx * w, sums[1] + dy * w, sums[2] + dz * w]
            for c in range(3):
                sums_ref[c, at, :] = sums[c]
        return decode(k + 1)

    def choose(low, high, halves, k, row, first, extra):
        if low == high:
            return run(low + FEWEST, halves, k, row, first)
        mid = (low + high) // 2
        return lax.cond(
            extra <= mid,
            lambda: choose(low, mid, halves, k, row, first, extra),
            lambda: choose(mid + 1, high, halves, k, row, first, extra),
        )

    def item(k, now):
        row, first, extra, both = now
        most = LEAF // STEP - FEWEST
        return lax.cond(
            both == 1,
            lambda: choose(0, most, 2, k, row, first, extra),
            lambda: choose(0, most, 1, k, row, first, extra),
        )

    begin = control_ref[0, ITEMS + stage]
    lax.fori_loop(begin, control_ref[0, ITEMS + stage + 1], item, decode(begin))


def block_of(ref):
    return lambda b: ref[b * 8 : b * 8 + 8, :]


def y_member(y_all, flip):
    y = lax.axis_index("oct") // 4
    return lambda b: y_all[y ^ flip, b * 8 : b * 8 + 8, :]


def near_one_kernel(control_ref, own, pair, wide_a, wide_b, sums_ref, target_ref, source_ref, masks_ref):
    spread_targets(own, target_ref)
    sums_ref[...] = jnp.zeros_like(sums_ref)
    bodies = [block_of(own), block_of(pair.at[other_core()]), block_of(wide_a), block_of(wide_b)]
    near_part(control_ref, target_ref, sums_ref, source_ref, masks_ref, bodies, 0)


def near_two_kernel(control_ref, wide_a, wide_b, mine, before, target_ref, sums_ref, source_ref, masks_ref):
    spread_targets(mine, target_ref)
    bodies = [block_of(wide_a), block_of(wide_b)]
    near_part(control_ref, target_ref, sums_ref, source_ref, masks_ref, bodies, 1)


def near_three_kernel(
    control_ref, far_ref, z_one, y_all, target_ref, before, sums_ref, hot_ref, keep_ref, fold_ref, ones_ref, source_ref, masks_ref
):
    bodies = [block_of(z_one), y_member(y_all, 1), y_member(y_all, 2)]
    near_part(control_ref, target_ref, sums_ref, source_ref, masks_ref, bodies, 2)
    members = lax.axis_size("oct")
    far_count = far_ref.shape[1]
    lanes = lax.broadcasted_iota(I32, (BLK * far_count, 128), 1)
    code = jnp.concatenate([jnp.broadcast_to(far_ref[:, v : v + 1], (BLK, 128)) for v in range(far_count)], axis=0)
    group, member, slot = code // (BLK * members), code // BLK % members, code % BLK
    row = member % 4 * 16 + member // 4 * 4
    fold_from = lax.broadcasted_iota(I32, (128, 128), 0)
    fold_to = lax.broadcasted_iota(I32, (128, 128), 1)
    for part, (at_row, low, width, base) in enumerate(
        ((row + group // 2, slot * SLOT + group % 2 * 8, 8, 0), (row + 3, slot * SLOT + group * 2, 2, 8))
    ):
        hot_ref[part] = (lanes == at_row).astype(F32).astype(jnp.bfloat16)
        keep_ref[part] = ((lanes >= low) & (lanes < low + width)).astype(F32)
        fold_ref[part] = (fold_from % width + base == fold_to).astype(F32).astype(jnp.bfloat16)
    k = lax.broadcasted_iota(I32, ones_ref.shape, 0)
    n = lax.broadcasted_iota(I32, ones_ref.shape, 1)
    ones_ref[...] = ((k % SLOT == n // 128) & (k < 3 * SLOT)).astype(F32).astype(jnp.bfloat16)


def three_parts(a):
    hi = a.astype(jnp.bfloat16)
    rest = a - hi.astype(F32)
    mid = rest.astype(jnp.bfloat16)
    return hi, mid, (rest - mid.astype(F32)).astype(jnp.bfloat16)


def last_kernel(
    control_ref, hot_ref, keep_ref, fold_ref, ones_ref, own, z_one, z_two, target_ref, before,
    out_ref, sums_ref, table_ref, rows_ref, source_ref, masks_ref, *, entries, far_count
):
    near_part(control_ref, target_ref, sums_ref, source_ref, masks_ref, [block_of(z_two)], 3)
    sums = []
    lane8 = lax.broadcasted_iota(I32, (LEAF, BLK), 1)
    for c in range(3):
        columns = jnp.zeros((LEAF, BLK), F32)
        for b in range(BLK):
            part = jnp.sum(sums_ref[c, b * LEAF : (b + 1) * LEAF, :], axis=1, keepdims=True)
            columns = jnp.where(lane8 == b, part, columns)
        sums.append(columns.T)
    table_ref[64:, :] = jnp.zeros((64, 128), F32)
    me = lax.axis_index("oct") % 4
    other = 3 - me
    n = z_one.shape[0] - BODY
    for place, rows in (
        (me, own[BODY:, :]),
        (me ^ 1, z_one[BODY:, :]),
        (other, z_two[BODY : BODY + n, :]),
        (other ^ 1, z_two[BODY + n :, :]),
    ):
        table_ref[pl.ds(pl.multiple_of(place * n, n), n), :] = rows
    table = jnp.concatenate(three_parts(table_ref[...]), axis=1)
    lhs, rhs = [], []
    for half in range(2):
        rows = jnp.dot(hot_ref[half], table, preferred_element_type=F32)
        for part in range(3):
            chosen = jnp.where(keep_ref[half] > 0.0, rows[:, part * 128 : (part + 1) * 128], 0.0)
            lhs.append(chosen.astype(jnp.bfloat16))
            rhs.append(fold_ref[half])
    folded = jnp.dot(jnp.concatenate(lhs, axis=1), jnp.concatenate(rhs, axis=0), preferred_element_type=F32)
    hi, mid, low = (part.astype(F32) for part in three_parts(folded))
    parts = (hi + pltpu.roll(mid, SLOT, 1) + pltpu.roll(low, 2 * SLOT, 1)).astype(jnp.bfloat16)
    spread = jnp.dot(parts, ones_ref[...], preferred_element_type=F32)
    x, y, z, _ = planes(own)
    for v in range(far_count):
        mass, cx, cy, cz, xx, yy, zz, xy, xz, yz = (
            jnp.concatenate([spread[v * BLK : (v + 1) * BLK, k * 128 : k * 128 + 128]] * 2, axis=1) for k in range(10)
        )
        rx, ry, rz = x - cx, y - cy, z - cz
        inv = lax.rsqrt(rx * rx + ry * ry + rz * rz + far_soft)
        inv2 = inv * inv
        inv3 = inv * inv2
        inv5 = inv3 * inv2
        inv7 = inv5 * inv2
        qx = xx * rx + xy * ry + xz * rz
        qy = xy * rx + yy * ry + yz * rz
        qz = xz * rx + yz * ry + zz * rz
        rqr = rx * qx + ry * qy + rz * qz
        radial = -mass * inv3 - 2.5 * rqr * inv7
        sums[0] += rx * radial + qx * inv5
        sums[1] += ry * radial + qy * inv5
        sums[2] += rz * radial + qz * inv5
    lane = lax.broadcasted_iota(I32, (1, LEAF), 1)
    grav = 1.0 / (entries * LEAF)
    for c in range(3):
        rows_ref[c] = sums[c] * grav
        for b in range(BLK):
            out_ref[c : c + 1, b * LEAF : (b + 1) * LEAF] = jnp.where(lane < control_ref[b, COUNT], rows_ref[c, b : b + 1, :], 0.0)


def sources(sets):
    return [pltpu.VMEM((sets * BODY, 128), F32), pltpu.SMEM((4,), I32)]


def params(mib):
    return pltpu.CompilerParams(vmem_limit_bytes=mib << 20)


def cost(flops):
    return pl.CostEstimate(flops=flops, bytes_accessed=1 << 18, transcendentals=0)


def mine_kernel(own, y_all, out_ref):
    out_ref[:BODY, :] = own[:BODY, :]
    for y in range(4):
        out_ref[BODY + 4 * y : BODY + 4 * y + 4, :] = y_all[y, BODY : BODY + 4, :]


def relay_kernel(mine, z_one, out_ref):
    n = z_one.shape[0] - BODY
    out_ref[:BODY, :] = z_one[:BODY, :]
    out_ref[BODY : BODY + n, :] = mine[BODY:, :]
    out_ref[BODY + n :, :] = z_one[BODY:, :]


def small_call(kernel, rows, *operands):
    return pl.pallas_call(
        kernel,
        out_shape=jax.ShapeDtypeStruct((rows, 128), F32),
        in_specs=[VMEM] * len(operands),
        out_specs=VMEM,
        compiler_params=params(2),
    )(*operands)


def exchange(payload, axis, flip):
    return lax.ppermute(payload, axis, [(i, flip(i)) for i in range(lax.axis_size(axis))])


def step(positions, masses, counts, near_list, far_list):
    wide_bits = lax.axis_size("wide").bit_length() - 1
    shape = (BODY + 8, 128)
    entries = near_list.shape[1]
    own, control = pl.pallas_call(
        pack_kernel,
        out_shape=[jax.ShapeDtypeStruct(shape, F32), jax.ShapeDtypeStruct((BLK, 128), I32)],
        in_specs=[HBM] * 4,
        out_specs=[VMEM, VMEM],
        scratch_shapes=[
            pltpu.SMEM(counts.shape, I32),
            pltpu.VMEM(positions.shape, F32),
            pltpu.VMEM((16, 128), F32),
            pltpu.VMEM(near_list.shape, I32),
            pltpu.SemaphoreType.DMA((4,)),
        ],
        compiler_params=params(4),
        name="pack",
    )(*(pltpu.with_memory_space_constraint(a, pltpu.HBM) for a in (counts, positions, masses.reshape(16, 128), near_list)))
    wide = []
    cores = [[i, i + 1] for i in range(0, lax.axis_size("wide"), 2)]
    pair = lax.all_gather(own, "wide", axis_index_groups=cores)
    for bit in range(1, wide_bits):
        wide.append(exchange(own, "wide", lambda i, bit=bit: i ^ (1 << bit)))
    message = pl.pallas_call(
        join_kernel,
        out_shape=jax.ShapeDtypeStruct((4, *shape), F32),
        in_specs=[VMEM] * (1 + wide_bits),
        out_specs=VMEM,
        compiler_params=params(4),
        name="join",
    )(own, pair, *wide)
    y_groups = [[z + 4 * y for y in range(4)] for z in range(4)]
    y_all = lax.all_to_all(message, "oct", 0, 0, axis_index_groups=y_groups)
    state = jax.ShapeDtypeStruct((3, BLK * LEAF, 128), F32)
    sums = pl.pallas_call(
        near_one_kernel,
        out_shape=state,
        in_specs=[SMEM] + [VMEM] * 4,
        out_specs=VMEM,
        scratch_shapes=[pltpu.VMEM(state.shape, F32), *sources(4)],
        compiler_params=params(8),
        cost_estimate=cost(20 << 20),
        name="near_one",
    )(control, own, pair, wide[0], wide[1])
    mine = small_call(mine_kernel, BODY + 16, own, y_all)
    z_one = exchange(mine, "oct", lambda i: i ^ 1)
    targets, sums = pl.pallas_call(
        near_two_kernel,
        out_shape=[state, state],
        in_specs=[SMEM] + [VMEM] * 4,
        out_specs=[VMEM, VMEM],
        scratch_shapes=sources(3),
        input_output_aliases={4: 1},
        compiler_params=params(8),
        cost_estimate=cost(20 << 20),
        name="near_two",
    )(control, *wide[2:], mine, sums)
    relay = small_call(relay_kernel, BODY + 32, mine, z_one)
    z_two = exchange(relay, "oct", lambda i: (i & ~3) | RELAY[i & 3])
    far_count = far_list.shape[1]
    picks = [
        jax.ShapeDtypeStruct((2, BLK * far_count, 128), jnp.bfloat16),
        jax.ShapeDtypeStruct((2, BLK * far_count, 128), F32),
        jax.ShapeDtypeStruct((2, 128, 128), jnp.bfloat16),
        jax.ShapeDtypeStruct((128, 10 * 128), jnp.bfloat16),
    ]
    sums, *picked = pl.pallas_call(
        near_three_kernel,
        out_shape=[state, *picks],
        in_specs=[SMEM] + [VMEM] * 5,
        out_specs=[VMEM] * 5,
        scratch_shapes=sources(3),
        input_output_aliases={5: 0},
        compiler_params=params(8),
        cost_estimate=cost(20 << 20),
        name="near_three",
    )(control, far_list, relay, y_all, targets, sums)
    return pl.pallas_call(
        functools.partial(last_kernel, entries=entries, far_count=far_count),
        out_shape=[jax.ShapeDtypeStruct(positions.shape, F32), state],
        in_specs=[SMEM] + [VMEM] * 9,
        out_specs=[VMEM, VMEM],
        scratch_shapes=[
            pltpu.VMEM((128, 128), F32),
            pltpu.VMEM((3, BLK, LEAF), F32),
            *sources(1),
        ],
        input_output_aliases={9: 1},
        compiler_params=params(8),
        cost_estimate=cost(20 << 20),
        name="last",
    )(control, *picked, mine, z_one, z_two, targets, sums)[0]


def solution(mesh):
    return jax.shard_map(
        step,
        mesh=mesh,
        in_specs=(
            P(None, ("wide", "oct")),
            P(("wide", "oct")),
            P(("wide", "oct")),
            P(("wide", "oct"), None),
            P(("wide", "oct"), None),
        ),
        out_specs=P(None, ("wide", "oct")),
        check_vma=False,
    )
```

```python
import functools

import jax
import jax.numpy as jnp
from jax import lax
from jax.experimental import pallas as pl
from jax.experimental.pallas import tpu as pltpu
from jax.sharding import PartitionSpec as P


near_soft = 0.01
far_soft = 0.25
BLK = 8
LEAF = 256
BODY = BLK * 8
STEP = 32
FEWEST = 3
SLOT = 16
F32 = jnp.float32
I32 = jnp.int32
VMEM = pl.BlockSpec(memory_space=pltpu.VMEM)
SMEM = pl.BlockSpec(memory_space=pltpu.SMEM)
HBM = pl.BlockSpec(memory_space=pltpu.HBM)
RELAY = (3, 2, 1, 0)
COUNT = 127
ITEMS = 64
STAGES = ((0, 5, 6), (7, 8, 9, 3, 4), (1, 3, 4), (2,))
PLACES = 64


def planes(ref):
    half = [[ref[pl.ds(h * 4 + c, BLK, stride=8), :] for h in range(2)] for c in range(4)]
    return [jnp.concatenate(pair, axis=1) for pair in half]


def pack_kernel(counts_hbm, pos_hbm, mass_hbm, near_hbm, out_ref, control_ref, counts_ref, pos_ref, mass_ref, near_ref, sems):
    moves = ((pos_hbm, pos_ref), (mass_hbm, mass_ref), (counts_hbm, counts_ref), (near_hbm, near_ref))
    copies = [pltpu.make_async_copy(src, dst, sems.at[i]) for i, (src, dst) in enumerate(moves)]
    for copy in copies:
        copy.start()
    for copy in copies:
        copy.wait()
    lane = lax.broadcasted_iota(I32, (1, 128), 1)
    for b in range(BLK):
        for half in range(2):
            row = b * 8 + half * 4
            at = b * LEAF + half * 128
            for c in range(3):
                out_ref[row + c : row + c + 1, :] = pos_ref[c : c + 1, at : at + 128]
            live = lane + half * 128 < counts_ref[b]
            out_ref[row + 3 : row + 4, :] = jnp.where(live, mass_ref[2 * b + half : 2 * b + half + 1, :], 0.0)
    x, y, z, m = planes(out_ref)

    def total(a):
        return jnp.sum(a, axis=1, keepdims=True)

    mass = total(m)
    cx, cy, cz = total(x * m) / mass, total(y * m) / mass, total(z * m) / mass
    dx, dy, dz = x - cx, y - cy, z - cz
    mx, my, mz = m * dx, m * dy, m * dz
    xx, yy, zz = total(mx * dx), total(my * dy), total(mz * dz)
    trace = xx + yy + zz
    first = [mass, cx, cy, cz, 3.0 * xx - trace, 3.0 * yy - trace, 3.0 * zz - trace, 3.0 * total(mx * dy)]
    last = [3.0 * total(mx * dz), 3.0 * total(my * dz)]
    lanes = lax.broadcasted_iota(I32, (BLK, 128), 1)
    blocks = lax.broadcasted_iota(I32, (BLK, 128), 0)

    def cell_row(columns):
        tile = jnp.zeros((BLK, 128), F32)
        for k, column in enumerate(columns):
            tile = jnp.where(lanes % SLOT == k, column, tile)
        return jnp.sum(jnp.where(lanes // SLOT == blocks, tile, 0.0), axis=0, keepdims=True)

    rows = jnp.where(blocks == 0, cell_row(first), 0.0)
    out_ref[BODY:, :] = jnp.where(blocks == 1, cell_row(last), rows)
    code = near_ref[...]
    entries = code.shape[1]
    stage = jnp.zeros_like(code)
    value = lax.broadcasted_iota(I32, code.shape, 0) * PLACES + code % BLK
    early = lax.axis_index("oct") % 4 < 2
    for number, names in enumerate(STAGES):
        for place, name in enumerate(names):
            mine = code // BLK == name
            if name in (3, 4):
                mine = mine & (early if number == 1 else jnp.logical_not(early))
            stage = jnp.where(mine, number, stage)
            value = value + jnp.where(mine, place * BLK, 0)

    def column(a):
        return jnp.concatenate([jnp.broadcast_to(a[:, v : v + 1], (BLK, 128)) for v in range(entries)], axis=0).astype(F32)

    stages = column(stage)
    items = BLK * entries
    down = lax.broadcasted_iota(I32, (items, 128), 0).astype(F32)
    across = lax.broadcasted_iota(I32, (items, 128), 1).astype(F32)
    key = stages * items + down
    rank = jnp.sum((key.T[:items, :] < key[:, :items]).astype(F32), axis=1, keepdims=True)
    sorted_items = jnp.where(rank == across, column(value), 0.0)
    starts = (stages < across - ITEMS).astype(F32)
    row = jnp.sum(jnp.where(across < ITEMS, sorted_items, starts), axis=0, keepdims=True).astype(I32)
    control = jnp.where(blocks == 0, row, 0)
    for b in range(BLK):
        control = jnp.where((blocks == b) & (lanes == COUNT), counts_ref[b], control)
    control_ref[...] = control


def other_core():
    return 1 - lax.axis_index("wide") % 2


def join_kernel(*refs):
    own, pair, *others, out_ref = refs
    sets = [own, pair.at[other_core()], *others]
    first = [ref[BODY : BODY + 1, :] for ref in sets]
    last = sum(pltpu.roll(jnp.broadcast_to(ref[BODY + 1 : BODY + 2, :], (8, 128)), 2 * g, 1) if g else jnp.broadcast_to(ref[BODY + 1 : BODY + 2, :], (8, 128)) for g, ref in enumerate(sets))
    at = lax.broadcasted_iota(I32, (8, 128), 0)
    tile = jnp.where(at == 3, last, 0.0)
    for g in range(0, len(sets), 2):
        pair = jnp.broadcast_to(first[g], (8, 128))
        if g + 1 < len(sets):
            pair = pair + pltpu.roll(jnp.broadcast_to(first[g + 1], (8, 128)), 8, 1)
        tile = jnp.where(at == g // 2, pair, tile)
    for k in range(out_ref.shape[0]):
        out_ref[k, :BODY, :] = sets[0][:BODY, :]
        out_ref[k, BODY:, :] = tile


def spread_targets(own, target_ref):
    k = lax.broadcasted_iota(I32, (3 * BLK, BLK * 128), 0)
    n = lax.broadcasted_iota(I32, (3 * BLK, BLK * 128), 1)
    ones = (k % BLK == n // 128).astype(F32).astype(jnp.bfloat16)
    for c, plane in enumerate(planes(own)[:3]):
        parts = jnp.concatenate([part.astype(F32) for part in three_parts(plane)], axis=0).astype(jnp.bfloat16)
        spread = lax.dot_general(parts, ones, (((0,), (0,)), ((), ())), preferred_element_type=F32)
        for b in range(BLK):
            target_ref[c, b * LEAF : (b + 1) * LEAF, :] = spread[:, b * 128 : (b + 1) * 128]


def near_part(control_ref, target_ref, sums_ref, source_ref, masks_ref, bodies, stage):
    lane8 = lax.broadcasted_iota(I32, (BLK, 128), 1)
    block8 = lax.broadcasted_iota(I32, (BLK, 128), 0)
    for s, body in enumerate(bodies):
        for b in range(BLK):
            source_ref[s * BODY + b * 8 : s * BODY + b * 8 + 8, :] = body(b)
    for s in range(len(bodies)):
        second = source_ref[pl.ds(s * BODY + 7, BLK, stride=8), :]
        masks_ref[s] = jnp.sum(jnp.where((lane8 == 0) & (second > 0.0), jnp.left_shift(1, block8), 0))

    last = jnp.int32(ITEMS - 1)

    def decode(k):
        value = control_ref[0, jnp.minimum(k, last)]
        b, place = value // PLACES, value % PLACES
        steps = (control_ref[b, COUNT] + STEP - 1) // STEP
        both = jnp.right_shift(masks_ref[place // BLK], place % BLK) % 2
        return place * 8, b * LEAF, jnp.maximum(steps - FEWEST, 0), both

    def run(steps, halves, k, row, first):
        s = [
            [jnp.broadcast_to(source_ref[pl.ds(row + 4 * h + c, 1), :], (8, 128)) for c in range(4)]
            for h in range(halves)
        ]
        first = pl.multiple_of(first, LEAF)
        for i in range(steps * STEP // 8):
            at = pl.ds(first + 8 * i, 8)
            t = [target_ref[c, at, :] for c in range(3)]
            sums = [sums_ref[c, at, :] for c in range(3)]
            for h in range(halves):
                dx, dy, dz = s[h][0] - t[0], s[h][1] - t[1], s[h][2] - t[2]
                inv = lax.rsqrt(dx * dx + dy * dy + dz * dz + near_soft)
                w = s[h][3] * (inv * inv * inv)
                sums = [sums[0] + dx * w, sums[1] + dy * w, sums[2] + dz * w]
            for c in range(3):
                sums_ref[c, at, :] = sums[c]
        return decode(k + 1)

    def choose(low, high, halves, k, row, first, extra):
        if low == high:
            return run(low + FEWEST, halves, k, row, first)
        mid = (low + high) // 2
        return lax.cond(
            extra <= mid,
            lambda: choose(low, mid, halves, k, row, first, extra),
            lambda: choose(mid + 1, high, halves, k, row, first, extra),
        )

    def item(k, now):
        row, first, extra, both = now
        most = LEAF // STEP - FEWEST
        return lax.cond(
            both == 1,
            lambda: choose(0, most, 2, k, row, first, extra),
            lambda: choose(0, most, 1, k, row, first, extra),
        )

    begin = control_ref[0, ITEMS + stage]
    lax.fori_loop(begin, control_ref[0, ITEMS + stage + 1], item, decode(begin))


def block_of(ref):
    return lambda b: ref[b * 8 : b * 8 + 8, :]


def y_member(y_all, flip):
    y = lax.axis_index("oct") // 4
    return lambda b: y_all[y ^ flip, b * 8 : b * 8 + 8, :]


def near_one_kernel(control_ref, own, pair, wide_a, sums_ref, target_ref, source_ref, masks_ref):
    spread_targets(own, target_ref)
    sums_ref[...] = jnp.zeros_like(sums_ref)
    bodies = [block_of(own), block_of(pair.at[other_core()]), block_of(wide_a)]
    near_part(control_ref, target_ref, sums_ref, source_ref, masks_ref, bodies, 0)


def near_two_kernel(control_ref, wide_a, wide_b, wide_c, y_all, mine, before, target_ref, sums_ref, source_ref, masks_ref):
    spread_targets(mine, target_ref)
    bodies = [*map(block_of, (wide_a, wide_b, wide_c)), y_member(y_all, 1), y_member(y_all, 2)]
    near_part(control_ref, target_ref, sums_ref, source_ref, masks_ref, bodies, 1)


def near_three_kernel(
    control_ref, far_ref, z_one, y_all, target_ref, before, sums_ref, hot_ref, keep_ref, fold_ref, ones_ref, source_ref, masks_ref
):
    bodies = [block_of(z_one), y_member(y_all, 1), y_member(y_all, 2)]
    near_part(control_ref, target_ref, sums_ref, source_ref, masks_ref, bodies, 2)
    members = lax.axis_size("oct")
    far_count = far_ref.shape[1]
    lanes = lax.broadcasted_iota(I32, (BLK * far_count, 128), 1)
    code = jnp.concatenate([jnp.broadcast_to(far_ref[:, v : v + 1], (BLK, 128)) for v in range(far_count)], axis=0)
    group, member, slot = code // (BLK * members), code // BLK % members, code % BLK
    row = member % 4 * 16 + member // 4 * 4
    fold_from = lax.broadcasted_iota(I32, (128, 128), 0)
    fold_to = lax.broadcasted_iota(I32, (128, 128), 1)
    for part, (at_row, low, width, base) in enumerate(
        ((row + group // 2, slot * SLOT + group % 2 * 8, 8, 0), (row + 3, slot * SLOT + group * 2, 2, 8))
    ):
        hot_ref[part] = (lanes == at_row).astype(F32).astype(jnp.bfloat16)
        keep_ref[part] = ((lanes >= low) & (lanes < low + width)).astype(F32)
        fold_ref[part] = (fold_from % width + base == fold_to).astype(F32).astype(jnp.bfloat16)
    k = lax.broadcasted_iota(I32, ones_ref.shape, 0)
    n = lax.broadcasted_iota(I32, ones_ref.shape, 1)
    ones_ref[...] = ((k % SLOT == n // 128) & (k < 3 * SLOT)).astype(F32).astype(jnp.bfloat16)


def three_parts(a):
    hi = a.astype(jnp.bfloat16)
    rest = a - hi.astype(F32)
    mid = rest.astype(jnp.bfloat16)
    return hi, mid, (rest - mid.astype(F32)).astype(jnp.bfloat16)


def last_kernel(
    control_ref, hot_ref, keep_ref, fold_ref, ones_ref, own, z_one, z_two, target_ref, before,
    out_ref, sums_ref, table_ref, rows_ref, source_ref, masks_ref, *, entries, far_count
):
    near_part(control_ref, target_ref, sums_ref, source_ref, masks_ref, [block_of(z_two)], 3)
    sums = []
    lane8 = lax.broadcasted_iota(I32, (LEAF, BLK), 1)
    for c in range(3):
        columns = jnp.zeros((LEAF, BLK), F32)
        for b in range(BLK):
            part = jnp.sum(sums_ref[c, b * LEAF : (b + 1) * LEAF, :], axis=1, keepdims=True)
            columns = jnp.where(lane8 == b, part, columns)
        sums.append(columns.T)
    table_ref[64:, :] = jnp.zeros((64, 128), F32)
    me = lax.axis_index("oct") % 4
    other = 3 - me
    n = z_one.shape[0] - BODY
    for place, rows in (
        (me, own[BODY:, :]),
        (me ^ 1, z_one[BODY:, :]),
        (other, z_two[BODY : BODY + n, :]),
        (other ^ 1, z_two[BODY + n :, :]),
    ):
        table_ref[pl.ds(pl.multiple_of(place * n, n), n), :] = rows
    table = jnp.concatenate(three_parts(table_ref[...]), axis=1)
    lhs, rhs = [], []
    for half in range(2):
        rows = jnp.dot(hot_ref[half], table, preferred_element_type=F32)
        for part in range(3):
            chosen = jnp.where(keep_ref[half] > 0.0, rows[:, part * 128 : (part + 1) * 128], 0.0)
            lhs.append(chosen.astype(jnp.bfloat16))
            rhs.append(fold_ref[half])
    folded = jnp.dot(jnp.concatenate(lhs, axis=1), jnp.concatenate(rhs, axis=0), preferred_element_type=F32)
    hi, mid, low = (part.astype(F32) for part in three_parts(folded))
    parts = (hi + pltpu.roll(mid, SLOT, 1) + pltpu.roll(low, 2 * SLOT, 1)).astype(jnp.bfloat16)
    spread = jnp.dot(parts, ones_ref[...], preferred_element_type=F32)
    x, y, z, _ = planes(own)
    for v in range(far_count):
        mass, cx, cy, cz, xx, yy, zz, xy, xz, yz = (
            jnp.concatenate([spread[v * BLK : (v + 1) * BLK, k * 128 : k * 128 + 128]] * 2, axis=1) for k in range(10)
        )
        rx, ry, rz = x - cx, y - cy, z - cz
        inv = lax.rsqrt(rx * rx + ry * ry + rz * rz + far_soft)
        inv2 = inv * inv
        inv3 = inv * inv2
        inv5 = inv3 * inv2
        inv7 = inv5 * inv2
        qx = xx * rx + xy * ry + xz * rz
        qy = xy * rx + yy * ry + yz * rz
        qz = xz * rx + yz * ry + zz * rz
        rqr = rx * qx + ry * qy + rz * qz
        radial = -mass * inv3 - 2.5 * rqr * inv7
        sums[0] += rx * radial + qx * inv5
        sums[1] += ry * radial + qy * inv5
        sums[2] += rz * radial + qz * inv5
    lane = lax.broadcasted_iota(I32, (1, LEAF), 1)
    grav = 1.0 / (entries * LEAF)
    for c in range(3):
        rows_ref[c] = sums[c] * grav
        for b in range(BLK):
            out_ref[c : c + 1, b * LEAF : (b + 1) * LEAF] = jnp.where(lane < control_ref[b, COUNT], rows_ref[c, b : b + 1, :], 0.0)


def sources(sets):
    return [pltpu.VMEM((sets * BODY, 128), F32), pltpu.SMEM((PLACES // BLK,), I32)]


def params(mib):
    return pltpu.CompilerParams(vmem_limit_bytes=mib << 20)


def cost(flops):
    return pl.CostEstimate(flops=flops, bytes_accessed=1 << 18, transcendentals=0)


def mine_kernel(own, y_all, out_ref):
    out_ref[:BODY, :] = own[:BODY, :]
    for y in range(4):
        out_ref[BODY + 4 * y : BODY + 4 * y + 4, :] = y_all[y, BODY : BODY + 4, :]


def relay_kernel(mine, z_one, out_ref):
    n = z_one.shape[0] - BODY
    out_ref[:BODY, :] = z_one[:BODY, :]
    out_ref[BODY : BODY + n, :] = mine[BODY:, :]
    out_ref[BODY + n :, :] = z_one[BODY:, :]


def small_call(kernel, rows, *operands):
    return pl.pallas_call(
        kernel,
        out_shape=jax.ShapeDtypeStruct((rows, 128), F32),
        in_specs=[VMEM] * len(operands),
        out_specs=VMEM,
        compiler_params=params(2),
    )(*operands)


def exchange(payload, axis, flip):
    return lax.ppermute(payload, axis, [(i, flip(i)) for i in range(lax.axis_size(axis))])


def step(positions, masses, counts, near_list, far_list):
    wide_bits = lax.axis_size("wide").bit_length() - 1
    shape = (BODY + 8, 128)
    entries = near_list.shape[1]
    own, control = pl.pallas_call(
        pack_kernel,
        out_shape=[jax.ShapeDtypeStruct(shape, F32), jax.ShapeDtypeStruct((BLK, 128), I32)],
        in_specs=[HBM] * 4,
        out_specs=[VMEM, VMEM],
        scratch_shapes=[
            pltpu.SMEM(counts.shape, I32),
            pltpu.VMEM(positions.shape, F32),
            pltpu.VMEM((16, 128), F32),
            pltpu.VMEM(near_list.shape, I32),
            pltpu.SemaphoreType.DMA((4,)),
        ],
        compiler_params=params(4),
        name="pack",
    )(*(pltpu.with_memory_space_constraint(a, pltpu.HBM) for a in (counts, positions, masses.reshape(16, 128), near_list)))
    wide = []
    cores = [[i, i + 1] for i in range(0, lax.axis_size("wide"), 2)]
    pair = lax.all_gather(own, "wide", axis_index_groups=cores)
    for bit in range(1, wide_bits):
        wide.append(exchange(own, "wide", lambda i, bit=bit: i ^ (1 << bit)))
    message = pl.pallas_call(
        join_kernel,
        out_shape=jax.ShapeDtypeStruct((4, *shape), F32),
        in_specs=[VMEM] * (1 + wide_bits),
        out_specs=VMEM,
        compiler_params=params(4),
        name="join",
    )(own, pair, *wide)
    y_groups = [[z + 4 * y for y in range(4)] for z in range(4)]
    y_all = lax.all_to_all(message, "oct", 0, 0, axis_index_groups=y_groups)
    state = jax.ShapeDtypeStruct((3, BLK * LEAF, 128), F32)
    sums = pl.pallas_call(
        near_one_kernel,
        out_shape=state,
        in_specs=[SMEM] + [VMEM] * 3,
        out_specs=VMEM,
        scratch_shapes=[pltpu.VMEM(state.shape, F32), *sources(3)],
        compiler_params=params(8),
        cost_estimate=cost(20 << 20),
        name="near_one",
    )(control, own, pair, wide[0])
    mine = small_call(mine_kernel, BODY + 16, own, y_all)
    z_one = exchange(mine, "oct", lambda i: i ^ 1)
    targets, sums = pl.pallas_call(
        near_two_kernel,
        out_shape=[state, state],
        in_specs=[SMEM] + [VMEM] * 6,
        out_specs=[VMEM, VMEM],
        scratch_shapes=sources(5),
        input_output_aliases={6: 1},
        compiler_params=params(8),
        cost_estimate=cost(20 << 20),
        name="near_two",
    )(control, *wide[1:], y_all, mine, sums)
    relay = small_call(relay_kernel, BODY + 32, mine, z_one)
    z_two = exchange(relay, "oct", lambda i: (i & ~3) | RELAY[i & 3])
    far_count = far_list.shape[1]
    picks = [
        jax.ShapeDtypeStruct((2, BLK * far_count, 128), jnp.bfloat16),
        jax.ShapeDtypeStruct((2, BLK * far_count, 128), F32),
        jax.ShapeDtypeStruct((2, 128, 128), jnp.bfloat16),
        jax.ShapeDtypeStruct((128, 10 * 128), jnp.bfloat16),
    ]
    sums, *picked = pl.pallas_call(
        near_three_kernel,
        out_shape=[state, *picks],
        in_specs=[SMEM] + [VMEM] * 5,
        out_specs=[VMEM] * 5,
        scratch_shapes=sources(3),
        input_output_aliases={5: 0},
        compiler_params=params(8),
        cost_estimate=cost(20 << 20),
        name="near_three",
    )(control, far_list, relay, y_all, targets, sums)
    return pl.pallas_call(
        functools.partial(last_kernel, entries=entries, far_count=far_count),
        out_shape=[jax.ShapeDtypeStruct(positions.shape, F32), state],
        in_specs=[SMEM] + [VMEM] * 9,
        out_specs=[VMEM, VMEM],
        scratch_shapes=[
            pltpu.VMEM((128, 128), F32),
            pltpu.VMEM((3, BLK, LEAF), F32),
            *sources(1),
        ],
        input_output_aliases={9: 1},
        compiler_params=params(8),
        cost_estimate=cost(20 << 20),
        name="last",
    )(control, *picked, mine, z_one, z_two, targets, sums)[0]


def solution(mesh):
    return jax.shard_map(
        step,
        mesh=mesh,
        in_specs=(
            P(None, ("wide", "oct")),
            P(("wide", "oct")),
            P(("wide", "oct")),
            P(("wide", "oct"), None),
            P(("wide", "oct"), None),
        ),
        out_specs=P(None, ("wide", "oct")),
        check_vma=False,
    )
```

```python
import functools

import jax
import jax.numpy as jnp
from jax import lax
from jax.experimental import pallas as pl
from jax.experimental.pallas import tpu as pltpu
from jax.sharding import PartitionSpec as P


near_soft = 0.01
far_soft = 0.25
BLK = 8
LEAF = 256
BODY = BLK * 8
STEP = 32
FEWEST = 3
SLOT = 16
F32 = jnp.float32
I32 = jnp.int32
VMEM = pl.BlockSpec(memory_space=pltpu.VMEM)
SMEM = pl.BlockSpec(memory_space=pltpu.SMEM)
HBM = pl.BlockSpec(memory_space=pltpu.HBM)
RELAY = (3, 2, 1, 0)
COUNT = 127
ITEMS = 64
STAGES = ((0, 5, 6), (7, 8, 9, 3, 4), (1, 3, 4, 7), (2,))
LATER = {3: (2, 3), 4: (2, 3), 7: (3,)}
PLACES = 64


def planes(ref):
    half = [[ref[pl.ds(h * 4 + c, BLK, stride=8), :] for h in range(2)] for c in range(4)]
    return [jnp.concatenate(pair, axis=1) for pair in half]


def pack_kernel(counts_hbm, pos_hbm, mass_hbm, near_hbm, out_ref, control_ref, counts_ref, pos_ref, mass_ref, near_ref, sems):
    moves = ((pos_hbm, pos_ref), (mass_hbm, mass_ref), (counts_hbm, counts_ref), (near_hbm, near_ref))
    copies = [pltpu.make_async_copy(src, dst, sems.at[i]) for i, (src, dst) in enumerate(moves)]
    for copy in copies:
        copy.start()
    for copy in copies:
        copy.wait()
    lane = lax.broadcasted_iota(I32, (1, 128), 1)
    for b in range(BLK):
        for half in range(2):
            row = b * 8 + half * 4
            at = b * LEAF + half * 128
            for c in range(3):
                out_ref[row + c : row + c + 1, :] = pos_ref[c : c + 1, at : at + 128]
            live = lane + half * 128 < counts_ref[b]
            out_ref[row + 3 : row + 4, :] = jnp.where(live, mass_ref[2 * b + half : 2 * b + half + 1, :], 0.0)
    x, y, z, m = planes(out_ref)

    def total(a):
        return jnp.sum(a, axis=1, keepdims=True)

    mass = total(m)
    cx, cy, cz = total(x * m) / mass, total(y * m) / mass, total(z * m) / mass
    dx, dy, dz = x - cx, y - cy, z - cz
    mx, my, mz = m * dx, m * dy, m * dz
    xx, yy, zz = total(mx * dx), total(my * dy), total(mz * dz)
    trace = xx + yy + zz
    first = [mass, cx, cy, cz, 3.0 * xx - trace, 3.0 * yy - trace, 3.0 * zz - trace, 3.0 * total(mx * dy)]
    last = [3.0 * total(mx * dz), 3.0 * total(my * dz)]
    lanes = lax.broadcasted_iota(I32, (BLK, 128), 1)
    blocks = lax.broadcasted_iota(I32, (BLK, 128), 0)

    def cell_row(columns):
        tile = jnp.zeros((BLK, 128), F32)
        for k, column in enumerate(columns):
            tile = jnp.where(lanes % SLOT == k, column, tile)
        return jnp.sum(jnp.where(lanes // SLOT == blocks, tile, 0.0), axis=0, keepdims=True)

    rows = jnp.where(blocks == 0, cell_row(first), 0.0)
    out_ref[BODY:, :] = jnp.where(blocks == 1, cell_row(last), rows)
    code = near_ref[...]
    entries = code.shape[1]
    stage = jnp.zeros_like(code)
    value = lax.broadcasted_iota(I32, code.shape, 0) * PLACES + code % BLK
    z_hi = lax.axis_index("oct") % 4
    for number, names in enumerate(STAGES):
        for place, name in enumerate(names):
            mine = code // BLK == name
            if name in LATER:
                later = functools.reduce(jnp.logical_or, [z_hi == z for z in LATER[name]])
                mine = mine & (later if number == 2 else jnp.logical_not(later))
            stage = jnp.where(mine, number, stage)
            value = value + jnp.where(mine, place * BLK, 0)

    def column(a):
        return jnp.concatenate([jnp.broadcast_to(a[:, v : v + 1], (BLK, 128)) for v in range(entries)], axis=0).astype(F32)

    stages = column(stage)
    items = BLK * entries
    down = lax.broadcasted_iota(I32, (items, 128), 0).astype(F32)
    across = lax.broadcasted_iota(I32, (items, 128), 1).astype(F32)
    key = stages * items + down
    rank = jnp.sum((key.T[:items, :] < key[:, :items]).astype(F32), axis=1, keepdims=True)
    sorted_items = jnp.where(rank == across, column(value), 0.0)
    starts = (stages < across - ITEMS).astype(F32)
    row = jnp.sum(jnp.where(across < ITEMS, sorted_items, starts), axis=0, keepdims=True).astype(I32)
    control = jnp.where(blocks == 0, row, 0)
    for b in range(BLK):
        control = jnp.where((blocks == b) & (lanes == COUNT), counts_ref[b], control)
    control_ref[...] = control


def other_core():
    return 1 - lax.axis_index("wide") % 2


def join_kernel(*refs):
    own, pair, *others, out_ref = refs
    sets = [own, pair.at[other_core()], *others]
    first = [ref[BODY : BODY + 1, :] for ref in sets]
    last = sum(pltpu.roll(jnp.broadcast_to(ref[BODY + 1 : BODY + 2, :], (8, 128)), 2 * g, 1) if g else jnp.broadcast_to(ref[BODY + 1 : BODY + 2, :], (8, 128)) for g, ref in enumerate(sets))
    at = lax.broadcasted_iota(I32, (8, 128), 0)
    tile = jnp.where(at == 3, last, 0.0)
    for g in range(0, len(sets), 2):
        pair = jnp.broadcast_to(first[g], (8, 128))
        if g + 1 < len(sets):
            pair = pair + pltpu.roll(jnp.broadcast_to(first[g + 1], (8, 128)), 8, 1)
        tile = jnp.where(at == g // 2, pair, tile)
    for k in range(out_ref.shape[0]):
        out_ref[k, :BODY, :] = sets[0][:BODY, :]
        out_ref[k, BODY:, :] = tile


def spread_targets(own, target_ref):
    k = lax.broadcasted_iota(I32, (3 * BLK, BLK * 128), 0)
    n = lax.broadcasted_iota(I32, (3 * BLK, BLK * 128), 1)
    ones = (k % BLK == n // 128).astype(F32).astype(jnp.bfloat16)
    for c, plane in enumerate(planes(own)[:3]):
        parts = jnp.concatenate([part.astype(F32) for part in three_parts(plane)], axis=0).astype(jnp.bfloat16)
        spread = lax.dot_general(parts, ones, (((0,), (0,)), ((), ())), preferred_element_type=F32)
        for b in range(BLK):
            target_ref[c, b * LEAF : (b + 1) * LEAF, :] = spread[:, b * 128 : (b + 1) * 128]


def near_part(control_ref, target_ref, sums_ref, source_ref, masks_ref, bodies, stage):
    lane8 = lax.broadcasted_iota(I32, (BLK, 128), 1)
    block8 = lax.broadcasted_iota(I32, (BLK, 128), 0)
    for s, body in enumerate(bodies):
        for b in range(BLK):
            source_ref[s * BODY + b * 8 : s * BODY + b * 8 + 8, :] = body(b)
    for s in range(len(bodies)):
        second = source_ref[pl.ds(s * BODY + 7, BLK, stride=8), :]
        masks_ref[s] = jnp.sum(jnp.where((lane8 == 0) & (second > 0.0), jnp.left_shift(1, block8), 0))

    last = jnp.int32(ITEMS - 1)

    def decode(k):
        value = control_ref[0, jnp.minimum(k, last)]
        b, place = value // PLACES, value % PLACES
        steps = (control_ref[b, COUNT] + STEP - 1) // STEP
        both = jnp.right_shift(masks_ref[place // BLK], place % BLK) % 2
        return place * 8, b * LEAF, jnp.maximum(steps - FEWEST, 0), both

    def run(steps, halves, k, row, first):
        s = [
            [jnp.broadcast_to(source_ref[pl.ds(row + 4 * h + c, 1), :], (8, 128)) for c in range(4)]
            for h in range(halves)
        ]
        first = pl.multiple_of(first, LEAF)
        for i in range(steps * STEP // 8):
            at = pl.ds(first + 8 * i, 8)
            t = [target_ref[c, at, :] for c in range(3)]
            sums = [sums_ref[c, at, :] for c in range(3)]
            for h in range(halves):
                dx, dy, dz = s[h][0] - t[0], s[h][1] - t[1], s[h][2] - t[2]
                inv = lax.rsqrt(dx * dx + dy * dy + dz * dz + near_soft)
                w = s[h][3] * (inv * inv * inv)
                sums = [sums[0] + dx * w, sums[1] + dy * w, sums[2] + dz * w]
            for c in range(3):
                sums_ref[c, at, :] = sums[c]
        return decode(k + 1)

    def choose(low, high, halves, k, row, first, extra):
        if low == high:
            return run(low + FEWEST, halves, k, row, first)
        mid = (low + high) // 2
        return lax.cond(
            extra <= mid,
            lambda: choose(low, mid, halves, k, row, first, extra),
            lambda: choose(mid + 1, high, halves, k, row, first, extra),
        )

    def item(k, now):
        row, first, extra, both = now
        most = LEAF // STEP - FEWEST
        return lax.cond(
            both == 1,
            lambda: choose(0, most, 2, k, row, first, extra),
            lambda: choose(0, most, 1, k, row, first, extra),
        )

    begin = control_ref[0, ITEMS + stage]
    lax.fori_loop(begin, control_ref[0, ITEMS + stage + 1], item, decode(begin))


def block_of(ref):
    return lambda b: ref[b * 8 : b * 8 + 8, :]


def y_member(y_all, flip):
    y = lax.axis_index("oct") // 4
    return lambda b: y_all[y ^ flip, b * 8 : b * 8 + 8, :]


def near_one_kernel(control_ref, own, pair, wide_a, sums_ref, target_ref, source_ref, masks_ref):
    spread_targets(own, target_ref)
    sums_ref[...] = jnp.zeros_like(sums_ref)
    bodies = [block_of(own), block_of(pair.at[other_core()]), block_of(wide_a)]
    near_part(control_ref, target_ref, sums_ref, source_ref, masks_ref, bodies, 0)


def near_two_kernel(control_ref, wide_a, wide_b, wide_c, y_all, mine, before, target_ref, sums_ref, source_ref, masks_ref):
    spread_targets(mine, target_ref)
    bodies = [*map(block_of, (wide_a, wide_b, wide_c)), y_member(y_all, 1), y_member(y_all, 2)]
    near_part(control_ref, target_ref, sums_ref, source_ref, masks_ref, bodies, 1)


def near_three_kernel(
    control_ref, far_ref, z_one, y_all, wide_a, target_ref, before,
    sums_ref, hot_ref, keep_ref, fold_ref, ones_ref, source_ref, masks_ref,
):
    bodies = [block_of(z_one), y_member(y_all, 1), y_member(y_all, 2), block_of(wide_a)]
    near_part(control_ref, target_ref, sums_ref, source_ref, masks_ref, bodies, 2)
    members = lax.axis_size("oct")
    far_count = far_ref.shape[1]
    lanes = lax.broadcasted_iota(I32, (BLK * far_count, 128), 1)
    code = jnp.concatenate([jnp.broadcast_to(far_ref[:, v : v + 1], (BLK, 128)) for v in range(far_count)], axis=0)
    group, member, slot = code // (BLK * members), code // BLK % members, code % BLK
    row = member % 4 * 16 + member // 4 * 4
    fold_from = lax.broadcasted_iota(I32, (128, 128), 0)
    fold_to = lax.broadcasted_iota(I32, (128, 128), 1)
    for part, (at_row, low, width, base) in enumerate(
        ((row + group // 2, slot * SLOT + group % 2 * 8, 8, 0), (row + 3, slot * SLOT + group * 2, 2, 8))
    ):
        hot_ref[part] = (lanes == at_row).astype(F32).astype(jnp.bfloat16)
        keep_ref[part] = ((lanes >= low) & (lanes < low + width)).astype(F32)
        fold_ref[part] = (fold_from % width + base == fold_to).astype(F32).astype(jnp.bfloat16)
    k = lax.broadcasted_iota(I32, ones_ref.shape, 0)
    n = lax.broadcasted_iota(I32, ones_ref.shape, 1)
    ones_ref[...] = ((k % SLOT == n // 128) & (k < 3 * SLOT)).astype(F32).astype(jnp.bfloat16)


def three_parts(a):
    hi = a.astype(jnp.bfloat16)
    rest = a - hi.astype(F32)
    mid = rest.astype(jnp.bfloat16)
    return hi, mid, (rest - mid.astype(F32)).astype(jnp.bfloat16)


def last_kernel(
    control_ref, hot_ref, keep_ref, fold_ref, ones_ref, own, z_one, z_two, target_ref, before,
    out_ref, sums_ref, table_ref, rows_ref, source_ref, masks_ref, *, entries, far_count
):
    near_part(control_ref, target_ref, sums_ref, source_ref, masks_ref, [block_of(z_two)], 3)
    sums = []
    lane8 = lax.broadcasted_iota(I32, (LEAF, BLK), 1)
    for c in range(3):
        columns = jnp.zeros((LEAF, BLK), F32)
        for b in range(BLK):
            part = jnp.sum(sums_ref[c, b * LEAF : (b + 1) * LEAF, :], axis=1, keepdims=True)
            columns = jnp.where(lane8 == b, part, columns)
        sums.append(columns.T)
    table_ref[64:, :] = jnp.zeros((64, 128), F32)
    me = lax.axis_index("oct") % 4
    other = 3 - me
    n = z_one.shape[0] - BODY
    for place, rows in (
        (me, own[BODY:, :]),
        (me ^ 1, z_one[BODY:, :]),
        (other, z_two[BODY : BODY + n, :]),
        (other ^ 1, z_two[BODY + n :, :]),
    ):
        table_ref[pl.ds(pl.multiple_of(place * n, n), n), :] = rows
    table = jnp.concatenate(three_parts(table_ref[...]), axis=1)
    lhs, rhs = [], []
    for half in range(2):
        rows = jnp.dot(hot_ref[half], table, preferred_element_type=F32)
        for part in range(3):
            chosen = jnp.where(keep_ref[half] > 0.0, rows[:, part * 128 : (part + 1) * 128], 0.0)
            lhs.append(chosen.astype(jnp.bfloat16))
            rhs.append(fold_ref[half])
    folded = jnp.dot(jnp.concatenate(lhs, axis=1), jnp.concatenate(rhs, axis=0), preferred_element_type=F32)
    hi, mid, low = (part.astype(F32) for part in three_parts(folded))
    parts = (hi + pltpu.roll(mid, SLOT, 1) + pltpu.roll(low, 2 * SLOT, 1)).astype(jnp.bfloat16)
    spread = jnp.dot(parts, ones_ref[...], preferred_element_type=F32)
    x, y, z, _ = planes(own)
    for v in range(far_count):
        mass, cx, cy, cz, xx, yy, zz, xy, xz, yz = (
            jnp.concatenate([spread[v * BLK : (v + 1) * BLK, k * 128 : k * 128 + 128]] * 2, axis=1) for k in range(10)
        )
        rx, ry, rz = x - cx, y - cy, z - cz
        inv = lax.rsqrt(rx * rx + ry * ry + rz * rz + far_soft)
        inv2 = inv * inv
        inv3 = inv * inv2
        inv5 = inv3 * inv2
        inv7 = inv5 * inv2
        qx = xx * rx + xy * ry + xz * rz
        qy = xy * rx + yy * ry + yz * rz
        qz = xz * rx + yz * ry + zz * rz
        rqr = rx * qx + ry * qy + rz * qz
        radial = -mass * inv3 - 2.5 * rqr * inv7
        sums[0] += rx * radial + qx * inv5
        sums[1] += ry * radial + qy * inv5
        sums[2] += rz * radial + qz * inv5
    lane = lax.broadcasted_iota(I32, (1, LEAF), 1)
    grav = 1.0 / (entries * LEAF)
    for c in range(3):
        rows_ref[c] = sums[c] * grav
        for b in range(BLK):
            out_ref[c : c + 1, b * LEAF : (b + 1) * LEAF] = jnp.where(lane < control_ref[b, COUNT], rows_ref[c, b : b + 1, :], 0.0)


def sources(sets):
    return [pltpu.VMEM((sets * BODY, 128), F32), pltpu.SMEM((PLACES // BLK,), I32)]


def params(mib):
    return pltpu.CompilerParams(vmem_limit_bytes=mib << 20)


def cost(flops):
    return pl.CostEstimate(flops=flops, bytes_accessed=1 << 18, transcendentals=0)


def mine_kernel(own, y_all, out_ref):
    out_ref[:BODY, :] = own[:BODY, :]
    for y in range(4):
        out_ref[BODY + 4 * y : BODY + 4 * y + 4, :] = y_all[y, BODY : BODY + 4, :]


def relay_kernel(mine, z_one, out_ref):
    n = z_one.shape[0] - BODY
    out_ref[:BODY, :] = z_one[:BODY, :]
    out_ref[BODY : BODY + n, :] = mine[BODY:, :]
    out_ref[BODY + n :, :] = z_one[BODY:, :]


def small_call(kernel, rows, *operands):
    return pl.pallas_call(
        kernel,
        out_shape=jax.ShapeDtypeStruct((rows, 128), F32),
        in_specs=[VMEM] * len(operands),
        out_specs=VMEM,
        compiler_params=params(2),
    )(*operands)


def exchange(payload, axis, flip):
    return lax.ppermute(payload, axis, [(i, flip(i)) for i in range(lax.axis_size(axis))])


def step(positions, masses, counts, near_list, far_list):
    wide_bits = lax.axis_size("wide").bit_length() - 1
    shape = (BODY + 8, 128)
    entries = near_list.shape[1]
    own, control = pl.pallas_call(
        pack_kernel,
        out_shape=[jax.ShapeDtypeStruct(shape, F32), jax.ShapeDtypeStruct((BLK, 128), I32)],
        in_specs=[HBM] * 4,
        out_specs=[VMEM, VMEM],
        scratch_shapes=[
            pltpu.SMEM(counts.shape, I32),
            pltpu.VMEM(positions.shape, F32),
            pltpu.VMEM((16, 128), F32),
            pltpu.VMEM(near_list.shape, I32),
            pltpu.SemaphoreType.DMA((4,)),
        ],
        compiler_params=params(4),
        name="pack",
    )(*(pltpu.with_memory_space_constraint(a, pltpu.HBM) for a in (counts, positions, masses.reshape(16, 128), near_list)))
    wide = []
    cores = [[i, i + 1] for i in range(0, lax.axis_size("wide"), 2)]
    pair = lax.all_gather(own, "wide", axis_index_groups=cores)
    for bit in range(1, wide_bits):
        wide.append(exchange(own, "wide", lambda i, bit=bit: i ^ (1 << bit)))
    message = pl.pallas_call(
        join_kernel,
        out_shape=jax.ShapeDtypeStruct((4, *shape), F32),
        in_specs=[VMEM] * (1 + wide_bits),
        out_specs=VMEM,
        compiler_params=params(4),
        name="join",
    )(own, pair, *wide)
    y_groups = [[z + 4 * y for y in range(4)] for z in range(4)]
    y_all = lax.all_to_all(message, "oct", 0, 0, axis_index_groups=y_groups)
    state = jax.ShapeDtypeStruct((3, BLK * LEAF, 128), F32)
    sums = pl.pallas_call(
        near_one_kernel,
        out_shape=state,
        in_specs=[SMEM] + [VMEM] * 3,
        out_specs=VMEM,
        scratch_shapes=[pltpu.VMEM(state.shape, F32), *sources(3)],
        compiler_params=params(8),
        cost_estimate=cost(20 << 20),
        name="near_one",
    )(control, own, pair, wide[0])
    mine = small_call(mine_kernel, BODY + 16, own, y_all)
    z_one = exchange(mine, "oct", lambda i: i ^ 1)
    targets, sums = pl.pallas_call(
        near_two_kernel,
        out_shape=[state, state],
        in_specs=[SMEM] + [VMEM] * 6,
        out_specs=[VMEM, VMEM],
        scratch_shapes=sources(5),
        input_output_aliases={6: 1},
        compiler_params=params(8),
        cost_estimate=cost(20 << 20),
        name="near_two",
    )(control, *wide[1:], y_all, mine, sums)
    relay = small_call(relay_kernel, BODY + 32, mine, z_one)
    z_two = exchange(relay, "oct", lambda i: (i & ~3) | RELAY[i & 3])
    far_count = far_list.shape[1]
    picks = [
        jax.ShapeDtypeStruct((2, BLK * far_count, 128), jnp.bfloat16),
        jax.ShapeDtypeStruct((2, BLK * far_count, 128), F32),
        jax.ShapeDtypeStruct((2, 128, 128), jnp.bfloat16),
        jax.ShapeDtypeStruct((128, 10 * 128), jnp.bfloat16),
    ]
    sums, *picked = pl.pallas_call(
        near_three_kernel,
        out_shape=[state, *picks],
        in_specs=[SMEM] + [VMEM] * 6,
        out_specs=[VMEM] * 5,
        scratch_shapes=sources(4),
        input_output_aliases={6: 0},
        compiler_params=params(8),
        cost_estimate=cost(20 << 20),
        name="near_three",
    )(control, far_list, relay, y_all, wide[1], targets, sums)
    return pl.pallas_call(
        functools.partial(last_kernel, entries=entries, far_count=far_count),
        out_shape=[jax.ShapeDtypeStruct(positions.shape, F32), state],
        in_specs=[SMEM] + [VMEM] * 9,
        out_specs=[VMEM, VMEM],
        scratch_shapes=[
            pltpu.VMEM((128, 128), F32),
            pltpu.VMEM((3, BLK, LEAF), F32),
            *sources(1),
        ],
        input_output_aliases={9: 1},
        compiler_params=params(8),
        cost_estimate=cost(20 << 20),
        name="last",
    )(control, *picked, mine, z_one, z_two, targets, sums)[0]


def solution(mesh):
    return jax.shard_map(
        step,
        mesh=mesh,
        in_specs=(
            P(None, ("wide", "oct")),
            P(("wide", "oct")),
            P(("wide", "oct")),
            P(("wide", "oct"), None),
            P(("wide", "oct"), None),
        ),
        out_specs=P(None, ("wide", "oct")),
        check_vma=False,
    )
```
